32 devices in a mesh: ctx: 4 (over z), head: 8 (over y, x, core).
Axes of the slice: x: 2, y: 2, z: 4, core: 2. Of those that a mesh axis runs over, the one named last changes fastest.
Arguments:
- inputs: bfloat16 [8, 64, 4096], P('head', None, 'ctx'), may hold values from -6 to 6
- dt: float32 [8, 4096], P('head', 'ctx'), may hold values from 0.03 to 0.3
- decay_rate: float32 [8], P('head'), may hold values from 0.0024414062 to 0.4, as said below
- skip: float32 [8], P('head'), may hold values from 0.5 to 1.5
- b_proj: bfloat16 [128, 4096], P(None, 'ctx'), may hold values from -1.1953125 to 1.1953125
- c_proj: bfloat16 [128, 4096], P(None, 'ctx'), may hold values from -1.1953125 to 1.1953125
- lengths: int32 [16], replicated, may hold values from 1 to 1024, 4096 in all
- grad_out: bfloat16 [8, 64, 4096], P('head', None, 'ctx'), may hold values from -0.59765625 to 0.59765625
Outputs:
- mixed: bfloat16 [8, 64, 4096], P('head', None, 'ctx')
- grad_inputs: bfloat16 [8, 64, 4096], P('head', None, 'ctx')
- grad_dt: float32 [8, 4096], P('head', 'ctx')
- grad_b: float32 [128, 4096], P('head', 'ctx')
- grad_c: float32 [128, 4096], P('head', 'ctx')
The draws below stay inside these ranges and needn't reach their ends.
Inputs may be any that keep to these rules, and one draw needn't show every extreme that they name: `decay_rate`: each head's decay rate is positive.
All inputs are finite; a program needn't handle non-finite values.
Results may differ from the reference program's by a relative error of at most 0.001.
Values sent between devices are 32-bit elements; how exact they have to be, the bound alone decides.
A program may use at most 64 MiB of HBM per device.

```python
import math
import jax
import jax.numpy as jnp
import numpy as np
from jax import lax

P_SIZE = 64
N = 128
BLOCK = 128
NDOC = 16
HEADS = 8
SEQ = 4096
DOC_MOST = 1024


def draw_decay_rate(key, part):
    key_slow, key_fast, key_pick = jax.random.split(key, 3)
    slow_rate = jnp.exp(jax.random.uniform(key_slow, (HEADS,), jnp.float32, jnp.log(10.0 / SEQ), jnp.log(60.0 / SEQ)))
    fast_rate = jnp.exp(jax.random.uniform(key_fast, (HEADS,), jnp.float32, jnp.log(0.1), jnp.log(0.4)))
    picked = jax.random.randint(key_pick, (HEADS,), 0, 2) == 1
    return jnp.where(picked, slow_rate, fast_rate).astype(jnp.float32)


def shard_levels(stream_key, shape, shards, low, largest):
    level, own = 1.0, jax.random.fold_in(stream_key, 6)
    for dim, parts in shards:
        draws = jnp.exp(jax.random.uniform(jax.random.fold_in(own, dim), (parts,), jnp.float32, low / len(shards), largest / len(shards)))
        level = level * jnp.repeat(draws, shape[dim] // parts).reshape([-1 if axis == dim else 1 for axis in range(len(shape))])
    return level


def split_up(number_of, total, limit, slope):
    weights = [(1 << 20) // math.isqrt(grade ** slope) + 1 for grade in range(2, number_of + 1)]
    surplus, holding = total - limit - (number_of - 1), [1] * (number_of - 1)
    while surplus > 0:
        candidates = [i for i in range(number_of - 1) if holding[i] < limit]
        mass, budget = sum([weights[i] for i in candidates]), surplus
        for i in candidates:
            extra = min(limit - holding[i], max(1, budget * weights[i] // mass), surplus)
            holding[i] = holding[i] + extra
            surplus = surplus - extra
    return np.array([limit] + holding)


def ragged_sizes(own_key, amount, total, bound, slope):
    if amount == 2:
        one = jax.random.randint(own_key, (), max(1, total - bound), min(bound, total - 1) + 1)
        return jnp.stack([one, total - one])
    sizes = jnp.asarray(split_up(amount, total, bound, slope), jnp.int32)
    pairs = (amount - 1) // 2
    giver, receiver = sizes[1:1 + 2 * pairs:2], sizes[2:2 + 2 * pairs:2]
    room = jnp.minimum(giver - 1, bound - receiver)
    moved = jax.random.randint(jax.random.fold_in(own_key, 1), (pairs,), 0, 1 << 20) % (room + 1)
    sizes = sizes.at[1:1 + 2 * pairs:2].set(giver - moved).at[2:2 + 2 * pairs:2].set(receiver + moved)
    return sizes[jax.random.permutation(jax.random.fold_in(own_key, 2), amount)]


def noise(own_key, dims, spread, most, cuts=(), held_as=jnp.bfloat16):
    loudness = shard_levels(own_key, dims, cuts, -0.22, 0.18) if cuts else 1.0
    entries = jax.random.normal(own_key, dims, jnp.float32) * spread * loudness
    return jnp.minimum(jnp.maximum(entries, -most), most).astype(held_as)


def setup_inputs(seed: int = 0) -> dict:
    keys = jax.random.split(jax.random.key(seed), 9)
    inputs = noise(keys[0], (HEADS, P_SIZE, SEQ), 1.0, 6.0, ((0, 8), (2, 4)))
    dt = jnp.clip(jnp.exp(math.log(0.3) - 2.3025852 * jax.random.uniform(keys[1], (HEADS, SEQ), jnp.float32) ** shard_levels(keys[1], (HEADS, SEQ), ((0, 8), (1, 4)), -0.2, 0.2)), 0.03, 0.3)
    decay_rate = draw_decay_rate(jax.random.fold_in(keys[8], 71), 0)
    skip = jnp.clip(0.5 + 1.0 * jax.random.uniform(keys[3], (HEADS,), jnp.float32) ** shard_levels(keys[3], (HEADS,), ((0, 8),), -0.2, 0.2), 0.5, 1.5)
    b_proj = noise(keys[4], (N, SEQ), 0.2, 1.1953125, ((1, 4),))
    c_proj = noise(keys[5], (N, SEQ), 0.2, 1.1953125, ((1, 4),))
    lengths = ragged_sizes(keys[6], NDOC, SEQ, DOC_MOST, 2).astype(jnp.int32)
    grad_out = noise(keys[7], (HEADS, P_SIZE, SEQ), 0.1, 0.59765625, ((0, 8), (2, 4)))
    return {"inputs": inputs, "dt": dt, "decay_rate": decay_rate, "skip": skip, "b_proj": b_proj, "c_proj": c_proj, "lengths": lengths, "grad_out": grad_out}


HIGH = lax.Precision.HIGHEST

def mixing_block(state_in, block_data, decay_rate, skip_gain, lower_ones):
    x_block, dt_block, b_block, c_block, seg_block, prev_seg = block_data
    log_decay = -decay_rate * dt_block
    cumulative = jnp.dot(lower_ones, log_decay, precision=HIGH)
    pair_mask = (seg_block[:, None] == seg_block[None, :]) & (lower_ones > 0)
    log_gap = jnp.where(pair_mask, cumulative[:, None] - cumulative[None, :], 0.0)
    decay_mat = jnp.where(pair_mask, jnp.exp(log_gap), 0.0)
    gram_mat = jnp.dot(c_block.T, b_block, precision=HIGH)
    scaled_in = x_block * dt_block[None, :]
    y_inner = jnp.dot(scaled_in, (gram_mat * decay_mat).T, precision=HIGH)
    decay_in = jnp.where(seg_block == prev_seg, jnp.exp(cumulative), 0.0)
    y_block = y_inner + jnp.dot(state_in, c_block, precision=HIGH) * decay_in[None, :] + skip_gain * x_block
    last_seg = seg_block[-1]
    weight_out = jnp.where(seg_block == last_seg, jnp.exp(cumulative[-1] - cumulative), 0.0)
    decay_all = jnp.where(last_seg == prev_seg, jnp.exp(cumulative[-1]), 0.0)
    state_out = decay_all * state_in + jnp.dot(scaled_in * weight_out[None, :], b_block.T, precision=HIGH)
    return (state_out, y_block)

def run_head(x_head, dt_head, b_vals, c_vals, segment, before_first, decay_rate, skip_gain, start_state, block_len):
    width_p = x_head.shape[0]
    width_n = b_vals.shape[0]
    block_count = x_head.shape[1] // block_len
    x_blocks = x_head.reshape(width_p, block_count, block_len).transpose(1, 0, 2)
    dt_blocks = dt_head.reshape(block_count, block_len)
    b_blocks = b_vals.reshape(width_n, block_count, block_len).transpose(1, 0, 2)
    c_blocks = c_vals.reshape(width_n, block_count, block_len).transpose(1, 0, 2)
    seg_blocks = segment.reshape(block_count, block_len)
    shifted = jnp.concatenate([before_first.reshape(1).astype(jnp.int32), segment[:-1].astype(jnp.int32)])
    prev_segs = shifted.reshape(block_count, block_len)[:, 0]
    lower_ones = (lax.broadcasted_iota(jnp.int32, (block_len, block_len), 0) >= lax.broadcasted_iota(jnp.int32, (block_len, block_len), 1)).astype(jnp.float32)

    def advance(carry_state, block_data):
        return mixing_block(carry_state, block_data, decay_rate, skip_gain, lower_ones)
    end_state, y_blocks = lax.scan(advance, start_state, (x_blocks, dt_blocks, b_blocks, c_blocks, seg_blocks, prev_segs))
    return (y_blocks.transpose(1, 0, 2).reshape(width_p, -1), end_state)

def reference(inputs, dt, decay_rate, skip, b_proj, c_proj, lengths, grad_out):
    doc_ends = jnp.cumsum(lengths).astype(jnp.int32)
    positions = jnp.arange(SEQ, dtype=jnp.int32)
    segment = lax.optimization_barrier(jnp.sum((positions[None, :] >= doc_ends[:-1, None]).astype(jnp.int32), axis=0)).astype(jnp.int32)
    before_first = jnp.full((), -1, jnp.int32)
    b_float = b_proj.astype(jnp.float32)
    c_float = c_proj.astype(jnp.float32)
    zero_state = jnp.zeros((P_SIZE, N), jnp.float32)

    def one_head(totals, head_data):
        x_head, dt_head, rate_head, skip_head, grad_head = head_data

        def forward(x_vals, dt_vals, b_vals, c_vals):
            return run_head(x_vals, dt_vals, b_vals, c_vals, segment, before_first, rate_head, skip_head, zero_state, BLOCK)[0]
        y_head, pull_back = jax.vjp(forward, x_head.astype(jnp.float32), dt_head, b_float, c_float)
        grad_x, grad_step, grad_bv, grad_cv = pull_back(grad_head.astype(jnp.float32))
        return ((totals[0] + grad_bv, totals[1] + grad_cv), (y_head.astype(jnp.bfloat16), grad_x.astype(jnp.bfloat16), grad_step))
    start_totals = (jnp.zeros((N, SEQ), jnp.float32), jnp.zeros((N, SEQ), jnp.float32))
    (grad_b, grad_c), (mixed, grad_inputs, grad_dt) = lax.scan(one_head, start_totals, (inputs, dt, decay_rate, skip, grad_out))
    return (mixed, grad_inputs, grad_dt, grad_b, grad_c)
```

```python
import functools
import jax
import jax.numpy as jnp
from jax import lax
from jax.experimental import pallas as pl
from jax.experimental.pallas import tpu as pltpu
from jax.sharding import PartitionSpec as P

Q = 128
HIGH = lax.Precision.HIGHEST
F32 = jnp.float32
BF16 = jnp.bfloat16
MESH = pl.DeviceIdType.MESH


def mm(a, b, ca, cb):
    return lax.dot_general(a, b, (((ca,), (cb,)), ((), ())), preferred_element_type=F32)


def split(v):
    hi = v.astype(BF16)
    return hi, (v - hi.astype(F32)).astype(BF16)


def lanes(a, b):
    return jnp.concatenate([a, b], axis=1)


def rows(a, b):
    return jnp.concatenate([a, b], axis=0)


def kernel(cfg, rate_ref, skip_ref, len_in, x_in, dt_in, b_in, c_in, g_in, *refs):
    n_ctx, n_head, hops, fused, ndoc = cfg
    mixed_ref, gx_ref, gdt_ref, gb_ref, gc_ref = refs[:5]
    len_ref, x_ref, dt_ref, b_ref, c_ref, g_ref, load_sem = refs[5:12]
    (s_ref, gz_ref, ddt_ref, out_s, out_g, in_s, in_g, ctx_send, ctx_recv) = refs[12:21]
    if fused:
        part, recv1, send2, recv2, s1_send, s1_recv, s2_send, s2_recv = refs[21:]
    width_p = x_ref.shape[1]
    local = x_ref.shape[2]
    width_n = b_ref.shape[0]
    blocks = local // Q
    me = lax.axis_index("ctx")
    head = lax.axis_index("head")
    chips = n_head // 2
    core = lax.rem(head, 2)
    chip = head // 2

    barrier = pltpu.get_barrier_semaphore()

    @pl.when(me > 0)
    def _():
        pl.semaphore_signal(barrier, inc=1, device_id={"ctx": me - 1}, device_id_type=MESH)

    @pl.when(me < n_ctx - 1)
    def _():
        pl.semaphore_signal(barrier, inc=1, device_id={"ctx": me + 1}, device_id_type=MESH)

    if fused:
        pl.semaphore_signal(
            barrier, inc=1, device_id={"head": chip * 2 + 1 - core}, device_id_type=MESH
        )
        for d in range(1, chips):
            to = lax.rem(chip + d, chips) * 2 + core
            pl.semaphore_signal(barrier, inc=1, device_id={"head": to}, device_id_type=MESH)

    pairs = (
        (len_in, len_ref),
        (dt_in, dt_ref),
        (x_in, x_ref),
        (b_in, b_ref),
        (g_in, g_ref),
        (c_in, c_ref),
    )
    loads = [
        pltpu.make_async_copy(src, dst, load_sem.at[i]) for i, (src, dst) in enumerate(pairs)
    ]
    for load in loads:
        load.start()
    len_load, dt_load, x_load, b_load, g_load, c_load = loads

    rate = rate_ref[0]
    skip = skip_ref[0]
    offset = me * local

    len_load.wait()
    ends = []
    total = len_ref[0]
    for j in range(ndoc - 1):
        ends.append(total)
        total = total + len_ref[j + 1]

    def segment_of(pos):
        seg = jnp.zeros(pos.shape, jnp.int32)
        for end in ends:
            seg = seg + (pos >= end).astype(jnp.int32)
        return seg

    pos8 = (
        offset
        + lax.broadcasted_iota(jnp.int32, (blocks, Q), 0) * Q
        + lax.broadcasted_iota(jnp.int32, (blocks, Q), 1)
    )
    pos_t = (
        offset
        + lax.broadcasted_iota(jnp.int32, (Q, blocks), 1) * Q
        + lax.broadcasted_iota(jnp.int32, (Q, blocks), 0)
    )
    seg8 = segment_of(pos8)
    seg_t = segment_of(pos_t)
    before8 = jnp.where(pos8 == 0, -1, segment_of(pos8 - 1))
    prev8 = before8[:, 0:1]
    last8 = seg8[:, Q - 1 : Q]

    dt_load.wait()
    dt8 = jnp.concatenate([dt_ref[0:1, k * Q : (k + 1) * Q] for k in range(blocks)], axis=0)
    row_i = lax.broadcasted_iota(jnp.int32, (Q, Q), 0)
    col_j = lax.broadcasted_iota(jnp.int32, (Q, Q), 1)
    lower = row_i >= col_j
    lower_ones = lower.astype(F32)
    log8 = -rate * dt8
    cum8 = lax.dot_general(
        log8, lower_ones, (((1,), (1,)), ((), ())), precision=HIGH, preferred_element_type=F32
    )
    cum_t = lax.dot_general(
        lower_ones, log8, (((1,), (1,)), ((), ())), precision=HIGH, preferred_element_type=F32
    )
    end8 = cum8[:, Q - 1 : Q]
    din8 = jnp.where(seg8 == prev8, jnp.exp(cum8), 0.0)
    wdt8 = jnp.where(seg8 == last8, jnp.exp(end8 - cum8), 0.0) * dt8
    dall8 = jnp.where(last8 == prev8, jnp.exp(end8), 0.0)

    def cut(ref, k):
        return ref[0, :, k * Q : (k + 1) * Q]

    def cut2(ref, k):
        return ref[:, k * Q : (k + 1) * Q]

    ahead = [None] * blocks
    prod = jnp.ones((1, 1), F32)
    for k in range(blocks):
        ahead[k] = prod
        prod = prod * dall8[k : k + 1]
    decay_dev = prod
    behind = [None] * blocks
    prod = jnp.ones((1, 1), F32)
    for k in reversed(range(blocks)):
        behind[k] = prod
        prod = prod * dall8[k : k + 1]

    @pl.when(me == 0)
    def _():
        in_s[...] = jnp.zeros_like(in_s)

    @pl.when(me == n_ctx - 1)
    def _():
        in_g[...] = jnp.zeros_like(in_g)

    peers = chips if fused else 0
    at_end = (me == 0) | (me == n_ctx - 1)

    def meet():
        @pl.when(at_end)
        def _():
            pl.semaphore_wait(barrier, peers + 1)

        @pl.when(jnp.logical_not(at_end))
        def _():
            pl.semaphore_wait(barrier, peers + 2)

    def ctx_copy(r, way):
        src, dst = (out_s, in_s) if way == 0 else (out_g, in_g)
        return pltpu.make_async_remote_copy(
            src_ref=src.at[r],
            dst_ref=dst.at[r],
            send_sem=ctx_send.at[r, way],
            recv_sem=ctx_recv.at[r, way],
            device_id={"ctx": me + 1 if way == 0 else me - 1},
            device_id_type=MESH,
        )

    def ctx_start(r, way):
        @pl.when(me < n_ctx - 1 if way == 0 else me > 0)
        def _():
            ctx_copy(r, way).start()

    def ctx_wait(r):
        @pl.when(me > 0)
        def _():
            ctx_copy(r, 0).wait_recv()

        @pl.when(me < n_ctx - 1)
        def _():
            ctx_copy(r, 1).wait_recv()

    def ctx_done(r):
        @pl.when(me < n_ctx - 1)
        def _():
            ctx_copy(r, 0).wait_send()

        @pl.when(me > 0)
        def _():
            ctx_copy(r, 1).wait_send()

    x_load.wait()
    b_load.wait()
    state = jnp.zeros((width_p, width_n), F32)
    for k in range(blocks):
        s_ref[k] = state
        b_k = cut2(b_ref, k)
        hi, lo = split(cut(x_ref, k).astype(F32) * wdt8[k : k + 1])
        state = dall8[k : k + 1] * state + mm(lanes(hi, lo), lanes(b_k, b_k), 1, 1)
    out_s[0] = state
    meet()
    ctx_start(0, 0)
    g_load.wait()
    c_load.wait()
    carry = jnp.zeros((width_p, width_n), F32)
    for k in reversed(range(blocks)):
        gz_ref[k] = carry
        c_k = cut2(c_ref, k)
        hi, lo = split(cut(g_ref, k).astype(F32) * din8[k : k + 1])
        carry = dall8[k : k + 1] * carry + mm(lanes(hi, lo), lanes(c_k, c_k), 1, 1)
    out_g[0] = carry
    ctx_start(0, 1)

    def put(k, way, value, add):
        if fused:
            each = width_n // n_head
            chunk, lo = k // 2, (k % 2) * Q
            for h in range(n_head):
                at = (chunk, h % 2, h // 2, slice(way * each, (way + 1) * each), slice(lo, lo + Q))
                piece = value[h * each : (h + 1) * each]
                part[at] = part[at] + piece if add else piece
        else:
            ref = (gb_ref, gc_ref)[way]
            at = (slice(None), slice(k * Q, (k + 1) * Q))
            ref[at] = ref[at] + value if add else value

    def intra_w(k):
        x_k, g_k, b_k, c_k = cut(x_ref, k), cut(g_ref, k), cut2(b_ref, k), cut2(c_ref, k)
        mask = lower & (seg_t[:, k : k + 1] == seg8[k : k + 1])
        gap = jnp.where(mask, cum_t[:, k : k + 1] - cum8[k : k + 1], 0.0)
        ddt = jnp.where(mask, jnp.exp(gap), 0.0) * dt8[k : k + 1]
        ddt_ref[k] = ddt
        w_hi, w_lo = split(mm(g_k, x_k, 0, 0) * ddt)
        put(k, 0, mm(lanes(c_k, c_k), rows(w_hi, w_lo), 1, 0), False)
        put(k, 1, mm(lanes(b_k, b_k), lanes(w_hi, w_lo), 1, 1), False)

    diffs, qs, tails = [None] * blocks, [None] * blocks, [None] * blocks

    def inter_w(k, state_in, grad_in):
        x_k, g_k = cut(x_ref, k), cut(g_ref, k)
        s_k = s_ref[k] + ahead[k] * state_in
        gz = gz_ref[k] + behind[k] * grad_in
        s_ref[k] = s_k
        gz_ref[k] = gz
        s_hi, s_lo = split(s_k)
        z_hi, z_lo = split(gz)
        put(k, 0, mm(rows(z_hi, z_lo), rows(x_k, x_k), 0, 0) * wdt8[k : k + 1], True)
        put(k, 1, mm(rows(s_hi, s_lo), rows(g_k, g_k), 0, 0) * din8[k : k + 1], True)

    def outer(k, state_in):
        x_k, g_k, b_k, c_k = cut(x_ref, k), cut(g_ref, k), cut2(b_ref, k), cut2(c_ref, k)
        s_k = s_ref[k]
        gz = gz_ref[k]
        s_end = s_ref[k + 1] if k + 1 < blocks else out_s[0] + decay_dev * state_in
        tails[k] = jnp.sum(jnp.sum(gz * s_end, axis=0, keepdims=True), axis=1, keepdims=True)
        a_hi, a_lo = split(mm(c_k, b_k, 0, 0) * ddt_ref[k])
        s_hi, s_lo = split(s_k)
        z_hi, z_lo = split(gz)
        din, wdt = din8[k : k + 1], wdt8[k : k + 1]
        y = mm(lanes(x_k, x_k), lanes(a_hi, a_lo), 1, 1)
        y = y + mm(lanes(s_hi, s_lo), rows(c_k, c_k), 1, 0) * din
        v = mm(lanes(g_k, g_k), rows(a_hi, a_lo), 1, 0)
        v = v + mm(lanes(z_hi, z_lo), rows(b_k, b_k), 1, 0) * wdt
        x_f, g_f = x_k.astype(F32), g_k.astype(F32)
        mixed_ref[0, :, k * Q : (k + 1) * Q] = (y + skip * x_f).astype(BF16)
        gx_ref[0, :, k * Q : (k + 1) * Q] = (v + skip * g_f).astype(BF16)
        q_k = jnp.sum(x_f * v, axis=0, keepdims=True)
        qs[k] = q_k
        diffs[k] = jnp.sum(g_f * y, axis=0, keepdims=True) - q_k

    def pair_copy(chunk):
        return pltpu.make_async_remote_copy(
            src_ref=part.at[chunk, 1 - core],
            dst_ref=recv1.at[chunk],
            send_sem=s1_send.at[chunk],
            recv_sem=s1_recv.at[chunk],
            device_id={"head": chip * 2 + 1 - core},
            device_id_type=MESH,
        )

    def chip_copy(chunk, d):
        to = lax.rem(chip + d, chips)
        return pltpu.make_async_remote_copy(
            src_ref=send2.at[chunk, to],
            dst_ref=recv2.at[chunk, d - 1],
            send_sem=s2_send.at[chunk, d - 1],
            recv_sem=s2_recv.at[chunk, d - 1],
            device_id={"head": to * 2 + core},
            device_id_type=MESH,
        )

    def second(chunk):
        pair_copy(chunk).wait_recv()
        send2[chunk] = part[chunk, core] + recv1[chunk]
        for d in range(1, chips):
            chip_copy(chunk, d).start()

    for k in range(blocks):
        intra_w(k)
    ctx_wait(0)
    for r in range(1, hops):
        out_s[r] = out_s[0] + decay_dev * in_s[r - 1]
        out_g[r] = out_g[0] + decay_dev * in_g[r - 1]
        ctx_start(r, 0)
        ctx_start(r, 1)
        ctx_wait(r)
    state_in = in_s[hops - 1]
    grad_in = in_g[hops - 1]
    for k in range(blocks):
        inter_w(k, state_in, grad_in)
        if fused and k % 2 == 1:
            pair_copy(k // 2).start()
    for k in range(blocks):
        if fused and k < blocks // 2:
            second(k)
        outer(k, state_in)

    q8 = jnp.concatenate(qs, axis=0)
    r8 = jnp.concatenate(diffs, axis=0)
    tail8 = jnp.concatenate(tails, axis=0)
    back8 = lax.dot_general(
        r8, lower_ones, (((1,), (0,)), ((), ())), precision=HIGH, preferred_element_type=F32
    )
    gdt8 = q8 / dt8 - rate * (back8 + tail8)
    for k in range(blocks):
        gdt_ref[0:1, k * Q : (k + 1) * Q] = gdt8[k : k + 1]

    for r in range(hops):
        ctx_done(r)
    if fused:
        each = width_n // n_head
        chunks = blocks // 2
        for chunk in range(chunks):
            total = send2[chunk, chip]
            for d in range(1, chips):
                chip_copy(chunk, d).wait_recv()
                total = total + recv2[chunk, d - 1]
            at = slice(chunk * 2 * Q, (chunk + 1) * 2 * Q)
            gb_ref[:, at] = total[:each]
            gc_ref[:, at] = total[each:]
        for chunk in range(chunks):
            pair_copy(chunk).wait_send()
            for d in range(1, chips):
                chip_copy(chunk, d).wait_send()


def move(*refs):
    count = (len(refs) - 1) // 2
    sem = refs[-1]
    copies = [pltpu.make_async_copy(refs[i], refs[count + i], sem.at[i]) for i in range(count)]
    for copy in copies:
        copy.start()
    for copy in copies:
        copy.wait()


def per_device(n_ctx, n_head, inputs, dt, decay_rate, skip, b_proj, c_proj, lengths, grad_out):
    _, width_p, local = inputs.shape
    width_n = b_proj.shape[0]
    longest = n_ctx * local // 4
    hops = max(1, min(n_ctx - 1, (longest - 2) // local + 1))
    each = width_n // n_head
    fused = each % 8 == 0
    blocks = local // Q
    chips = n_head // 2
    chunks = blocks // 2
    vmem = pl.BlockSpec(memory_space=pltpu.VMEM)
    smem = pl.BlockSpec(memory_space=pltpu.SMEM)
    anywhere = pl.BlockSpec(memory_space=pl.ANY)
    result = pltpu.VMEM if fused else jax.ShapeDtypeStruct
    grad_rows = each if fused else width_n
    scratch = [
        pltpu.SMEM(lengths.shape, lengths.dtype),
        pltpu.VMEM(inputs.shape, BF16),
        pltpu.VMEM(dt.shape, F32),
        pltpu.VMEM(b_proj.shape, BF16),
        pltpu.VMEM(c_proj.shape, BF16),
        pltpu.VMEM(grad_out.shape, BF16),
        pltpu.SemaphoreType.DMA((6,)),
        pltpu.VMEM((blocks, width_p, width_n), F32),
        pltpu.VMEM((blocks, width_p, width_n), F32),
        pltpu.VMEM((blocks, Q, Q), F32),
        pltpu.VMEM((hops, width_p, width_n), F32),
        pltpu.VMEM((hops, width_p, width_n), F32),
        pltpu.VMEM((hops, width_p, width_n), F32),
        pltpu.VMEM((hops, width_p, width_n), F32),
        pltpu.SemaphoreType.DMA((hops, 2)),
        pltpu.SemaphoreType.DMA((hops, 2)),
    ]
    if fused:
        scratch += [
            pltpu.VMEM((chunks, 2, chips, 2 * each, 2 * Q), F32),
            pltpu.VMEM((chunks, chips, 2 * each, 2 * Q), F32),
            pltpu.VMEM((chunks, chips, 2 * each, 2 * Q), F32),
            pltpu.VMEM((chunks, chips - 1, 2 * each, 2 * Q), F32),
            pltpu.SemaphoreType.DMA((chunks,)),
            pltpu.SemaphoreType.DMA((chunks,)),
            pltpu.SemaphoreType.DMA((chunks, chips - 1)),
            pltpu.SemaphoreType.DMA((chunks, chips - 1)),
        ]
    mixed, gx, gdt, gb, gc = pl.pallas_call(
        functools.partial(kernel, (n_ctx, n_head, hops, fused, lengths.shape[0])),
        out_shape=(
            result(inputs.shape, BF16),
            result(inputs.shape, BF16),
            result(dt.shape, F32),
            result((grad_rows, local), F32),
            result((grad_rows, local), F32),
        ),
        in_specs=[smem, smem] + [anywhere] * 6,
        out_specs=(vmem,) * 5,
        scratch_shapes=scratch,
        compiler_params=pltpu.CompilerParams(collective_id=0, has_side_effects=True),
    )(decay_rate, skip, lengths, inputs, dt, b_proj, c_proj, grad_out)
    if not fused:
        gb = lax.psum_scatter(gb, "head", scatter_dimension=0, tiled=True)
        gc = lax.psum_scatter(gc, "head", scatter_dimension=0, tiled=True)
    results = (mixed, gx, gdt, gb, gc)
    if fused:
        results = tuple(pltpu.with_memory_space_constraint(r, pltpu.VMEM) for r in results)
    return pl.pallas_call(
        move,
        out_shape=tuple(jax.ShapeDtypeStruct(r.shape, r.dtype) for r in results),
        in_specs=[vmem if fused else anywhere] * 5,
        out_specs=(anywhere,) * 5,
        scratch_shapes=[pltpu.SemaphoreType.DMA((5,))],
    )(*results)


def solution(mesh):
    return jax.shard_map(
        functools.partial(per_device, mesh.shape["ctx"], mesh.shape["head"]),
        mesh=mesh,
        in_specs=(
            P("head", None, "ctx"),
            P("head", "ctx"),
            P("head"),
            P("head"),
            P(None, "ctx"),
            P(None, "ctx"),
            P(),
            P("head", None, "ctx"),
        ),
        out_specs=(
            P("head", None, "ctx"),
            P("head", None, "ctx"),
            P("head", "ctx"),
            P("head", "ctx"),
            P("head", "ctx"),
        ),
        check_vma=False,
    )
```

```python
import functools
import jax
import jax.numpy as jnp
from jax import lax
from jax.experimental import pallas as pl
from jax.experimental.pallas import tpu as pltpu
from jax.sharding import PartitionSpec as P

Q = 128
DIRECT = 2
HIGH = lax.Precision.HIGHEST
F32 = jnp.float32
BF16 = jnp.bfloat16
MESH = pl.DeviceIdType.MESH


def mm(a, b, ca, cb):
    return lax.dot_general(a, b, (((ca,), (cb,)), ((), ())), preferred_element_type=F32)


def split(v):
    hi = v.astype(BF16)
    return hi, (v - hi.astype(F32)).astype(BF16)


def lanes(a, b):
    return jnp.concatenate([a, b], axis=1)


def rows(a, b):
    return jnp.concatenate([a, b], axis=0)


def kernel(cfg, rate_ref, skip_ref, len_in, x_in, dt_in, b_in, c_in, g_in, *refs):
    n_ctx, n_head, hops, fused, ndoc = cfg
    mixed_ref, gx_ref, gdt_ref, gb_ref, gc_ref = refs[:5]
    len_ref, x_ref, dt_ref, b_ref, c_ref, g_ref, load_sem = refs[5:12]
    (s_ref, gz_ref, ddt_ref, out_s, out_g, in_s, in_g, ctx_send, ctx_recv) = refs[12:21]
    if fused:
        part, recv1, send2, recv2, hop1_out, hop1_in, hop2_out, hop2_in = refs[21:29]
        s1_send, s1_recv, s2_send, s2_recv = refs[29:]
    width_p = x_ref.shape[1]
    local = x_ref.shape[2]
    width_n = b_ref.shape[0]
    blocks = local // Q
    me = lax.axis_index("ctx")
    head = lax.axis_index("head")
    chips = n_head // 2
    core = lax.rem(head, 2)
    chip = head // 2

    barrier = pltpu.get_barrier_semaphore()

    @pl.when(me > 0)
    def _():
        pl.semaphore_signal(barrier, inc=1, device_id={"ctx": me - 1}, device_id_type=MESH)

    @pl.when(me < n_ctx - 1)
    def _():
        pl.semaphore_signal(barrier, inc=1, device_id={"ctx": me + 1}, device_id_type=MESH)

    if fused:
        pl.semaphore_signal(
            barrier, inc=1, device_id={"head": chip * 2 + 1 - core}, device_id_type=MESH
        )
        for d in range(1, chips):
            to = lax.rem(chip + d, chips) * 2 + core
            pl.semaphore_signal(barrier, inc=1, device_id={"head": to}, device_id_type=MESH)

    pairs = (
        (len_in, len_ref),
        (dt_in, dt_ref),
        (x_in, x_ref),
        (b_in, b_ref),
        (g_in, g_ref),
        (c_in, c_ref),
    )
    loads = [
        pltpu.make_async_copy(src, dst, load_sem.at[i]) for i, (src, dst) in enumerate(pairs)
    ]
    for load in loads:
        load.start()
    len_load, dt_load, x_load, b_load, g_load, c_load = loads

    rate = rate_ref[0]
    skip = skip_ref[0]
    offset = me * local

    len_load.wait()
    ends = []
    total = len_ref[0]
    for j in range(ndoc - 1):
        ends.append(total)
        total = total + len_ref[j + 1]

    def segment_of(pos):
        seg = jnp.zeros(pos.shape, jnp.int32)
        for end in ends:
            seg = seg + (pos >= end).astype(jnp.int32)
        return seg

    pos8 = (
        offset
        + lax.broadcasted_iota(jnp.int32, (blocks, Q), 0) * Q
        + lax.broadcasted_iota(jnp.int32, (blocks, Q), 1)
    )
    pos_t = (
        offset
        + lax.broadcasted_iota(jnp.int32, (Q, blocks), 1) * Q
        + lax.broadcasted_iota(jnp.int32, (Q, blocks), 0)
    )
    seg8 = segment_of(pos8)
    seg_t = segment_of(pos_t)
    before8 = jnp.where(pos8 == 0, -1, segment_of(pos8 - 1))
    prev8 = before8[:, 0:1]
    last8 = seg8[:, Q - 1 : Q]

    dt_load.wait()
    dt8 = jnp.concatenate([dt_ref[0:1, k * Q : (k + 1) * Q] for k in range(blocks)], axis=0)
    row_i = lax.broadcasted_iota(jnp.int32, (Q, Q), 0)
    col_j = lax.broadcasted_iota(jnp.int32, (Q, Q), 1)
    lower = row_i >= col_j
    lower_ones = lower.astype(F32)
    log8 = -rate * dt8
    cum8 = lax.dot_general(
        log8, lower_ones, (((1,), (1,)), ((), ())), precision=HIGH, preferred_element_type=F32
    )
    cum_t = lax.dot_general(
        lower_ones, log8, (((1,), (1,)), ((), ())), precision=HIGH, preferred_element_type=F32
    )
    end8 = cum8[:, Q - 1 : Q]
    din8 = jnp.where(seg8 == prev8, jnp.exp(cum8), 0.0)
    wdt8 = jnp.where(seg8 == last8, jnp.exp(end8 - cum8), 0.0) * dt8
    dall8 = jnp.where(last8 == prev8, jnp.exp(end8), 0.0)

    def cut(ref, k):
        return ref[0, :, k * Q : (k + 1) * Q]

    def cut2(ref, k):
        return ref[:, k * Q : (k + 1) * Q]

    ahead = [None] * blocks
    prod = jnp.ones((1, 1), F32)
    for k in range(blocks):
        ahead[k] = prod
        prod = prod * dall8[k : k + 1]
    decay_dev = prod
    behind = [None] * blocks
    prod = jnp.ones((1, 1), F32)
    for k in reversed(range(blocks)):
        behind[k] = prod
        prod = prod * dall8[k : k + 1]

    @pl.when(me == 0)
    def _():
        in_s[...] = jnp.zeros_like(in_s)

    @pl.when(me == n_ctx - 1)
    def _():
        in_g[...] = jnp.zeros_like(in_g)

    peers = chips if fused else 0
    at_end = (me == 0) | (me == n_ctx - 1)

    def meet():
        @pl.when(at_end)
        def _():
            pl.semaphore_wait(barrier, peers + 1)

        @pl.when(jnp.logical_not(at_end))
        def _():
            pl.semaphore_wait(barrier, peers + 2)

    def ctx_copy(r, way):
        src, dst = (out_s, in_s) if way == 0 else (out_g, in_g)
        return pltpu.make_async_remote_copy(
            src_ref=src.at[r],
            dst_ref=dst.at[r],
            send_sem=ctx_send.at[r, way],
            recv_sem=ctx_recv.at[r, way],
            device_id={"ctx": me + 1 if way == 0 else me - 1},
            device_id_type=MESH,
        )

    def ctx_start(r, way):
        @pl.when(me < n_ctx - 1 if way == 0 else me > 0)
        def _():
            ctx_copy(r, way).start()

    def ctx_wait(r):
        @pl.when(me > 0)
        def _():
            ctx_copy(r, 0).wait_recv()

        @pl.when(me < n_ctx - 1)
        def _():
            ctx_copy(r, 1).wait_recv()

    def ctx_done(r):
        @pl.when(me < n_ctx - 1)
        def _():
            ctx_copy(r, 0).wait_send()

        @pl.when(me > 0)
        def _():
            ctx_copy(r, 1).wait_send()

    x_load.wait()
    b_load.wait()
    state = jnp.zeros((width_p, width_n), F32)
    for k in range(blocks):
        s_ref[k] = state
        b_k = cut2(b_ref, k)
        hi, lo = split(cut(x_ref, k).astype(F32) * wdt8[k : k + 1])
        state = dall8[k : k + 1] * state + mm(lanes(hi, lo), lanes(b_k, b_k), 1, 1)
    out_s[0] = state
    meet()
    ctx_start(0, 0)
    g_load.wait()
    c_load.wait()
    carry = jnp.zeros((width_p, width_n), F32)
    for k in reversed(range(blocks)):
        gz_ref[k] = carry
        c_k = cut2(c_ref, k)
        hi, lo = split(cut(g_ref, k).astype(F32) * din8[k : k + 1])
        carry = dall8[k : k + 1] * carry + mm(lanes(hi, lo), lanes(c_k, c_k), 1, 1)
    out_g[0] = carry
    ctx_start(0, 1)

    def put(k, way, value, add):
        if fused:
            each = width_n // n_head
            chunk, lo = k // 2, (k % 2) * Q
            for h in range(n_head):
                at = (chunk, h % 2, h // 2, slice(way * each, (way + 1) * each), slice(lo, lo + Q))
                piece = value[h * each : (h + 1) * each]
                part[at] = part[at] + piece if add else piece
        else:
            ref = (gb_ref, gc_ref)[way]
            at = (slice(None), slice(k * Q, (k + 1) * Q))
            ref[at] = ref[at] + value if add else value

    def intra_w(k):
        x_k, g_k, b_k, c_k = cut(x_ref, k), cut(g_ref, k), cut2(b_ref, k), cut2(c_ref, k)
        mask = lower & (seg_t[:, k : k + 1] == seg8[k : k + 1])
        gap = jnp.where(mask, cum_t[:, k : k + 1] - cum8[k : k + 1], 0.0)
        ddt = jnp.where(mask, jnp.exp(gap), 0.0) * dt8[k : k + 1]
        ddt_ref[k] = ddt
        w_hi, w_lo = split(mm(g_k, x_k, 0, 0) * ddt)
        put(k, 0, mm(lanes(c_k, c_k), rows(w_hi, w_lo), 1, 0), False)
        put(k, 1, mm(lanes(b_k, b_k), lanes(w_hi, w_lo), 1, 1), False)

    diffs, qs, tails = [None] * blocks, [None] * blocks, [None] * blocks

    def inter_w(k, state_in, grad_in):
        x_k, g_k = cut(x_ref, k), cut(g_ref, k)
        s_k = s_ref[k] + ahead[k] * state_in
        gz = gz_ref[k] + behind[k] * grad_in
        s_ref[k] = s_k
        gz_ref[k] = gz
        s_hi, s_lo = split(s_k)
        z_hi, z_lo = split(gz)
        put(k, 0, mm(rows(z_hi, z_lo), rows(x_k, x_k), 0, 0) * wdt8[k : k + 1], True)
        put(k, 1, mm(rows(s_hi, s_lo), rows(g_k, g_k), 0, 0) * din8[k : k + 1], True)

    def outer(k, state_in):
        x_k, g_k, b_k, c_k = cut(x_ref, k), cut(g_ref, k), cut2(b_ref, k), cut2(c_ref, k)
        s_k = s_ref[k]
        gz = gz_ref[k]
        s_end = s_ref[k + 1] if k + 1 < blocks else out_s[0] + decay_dev * state_in
        tails[k] = jnp.sum(jnp.sum(gz * s_end, axis=0, keepdims=True), axis=1, keepdims=True)
        a_hi, a_lo = split(mm(c_k, b_k, 0, 0) * ddt_ref[k])
        s_hi, s_lo = split(s_k)
        z_hi, z_lo = split(gz)
        din, wdt = din8[k : k + 1], wdt8[k : k + 1]
        y = mm(lanes(x_k, x_k), lanes(a_hi, a_lo), 1, 1)
        y = y + mm(lanes(s_hi, s_lo), rows(c_k, c_k), 1, 0) * din
        v = mm(lanes(g_k, g_k), rows(a_hi, a_lo), 1, 0)
        v = v + mm(lanes(z_hi, z_lo), rows(b_k, b_k), 1, 0) * wdt
        x_f, g_f = x_k.astype(F32), g_k.astype(F32)
        mixed_ref[0, :, k * Q : (k + 1) * Q] = (y + skip * x_f).astype(BF16)
        gx_ref[0, :, k * Q : (k + 1) * Q] = (v + skip * g_f).astype(BF16)
        q_k = jnp.sum(x_f * v, axis=0, keepdims=True)
        qs[k] = q_k
        diffs[k] = jnp.sum(g_f * y, axis=0, keepdims=True) - q_k

    def pair_copy(chunk):
        return pltpu.make_async_remote_copy(
            src_ref=part.at[chunk, 1 - core],
            dst_ref=recv1.at[chunk],
            send_sem=s1_send.at[chunk],
            recv_sem=s1_recv.at[chunk],
            device_id={"head": chip * 2 + 1 - core},
            device_id_type=MESH,
        )

    def chip_copy(chunk, d):
        to = lax.rem(chip + d, chips)
        return pltpu.make_async_remote_copy(
            src_ref=send2.at[chunk, to],
            dst_ref=recv2.at[chunk, d - 1],
            send_sem=s2_send.at[chunk, d - 1],
            recv_sem=s2_recv.at[chunk, d - 1],
            device_id={"head": to * 2 + core},
            device_id_type=MESH,
        )

    def hop_copy(chunk, hop, way):
        src, dst = (hop1_out, hop1_in) if hop == 0 else (hop2_out, hop2_in)
        to = chip ^ (1 + (way + hop) % 2)
        return pltpu.make_async_remote_copy(
            src_ref=src.at[chunk, way],
            dst_ref=dst.at[chunk, way],
            send_sem=s2_send.at[chunk, 2 * hop + way],
            recv_sem=s2_recv.at[chunk, 2 * hop + way],
            device_id={"head": to * 2 + core},
            device_id_type=MESH,
        )

    each = width_n // n_head

    def paired(chunk, to, way):
        at = slice(way * each, (way + 1) * each)
        return part[chunk, core, to, at] + recv1[chunk, to, at]

    def in_two_hops(chunk):
        return chips == 4 and chunk < blocks // 2 - DIRECT

    def second(chunk):
        pair_copy(chunk).wait_recv()
        if in_two_hops(chunk):
            for way in range(2):
                hop1_out[chunk, way, 0] = paired(chunk, chip ^ (1 + way), way)
                hop1_out[chunk, way, 1] = paired(chunk, chip ^ 3, way)
                hop_copy(chunk, 0, way).start()
        else:
            send2[chunk] = part[chunk, core] + recv1[chunk]
            for d in range(1, chips):
                chip_copy(chunk, d).start()

    def third(chunk):
        for way in range(2):
            hop_copy(chunk, 0, way).wait_recv()
            hop2_out[chunk, way] = paired(chunk, chip ^ (2 - way), way) + hop1_in[chunk, way, 1]
            hop_copy(chunk, 1, way).start()

    def last(chunk):
        at = slice(chunk * 2 * Q, (chunk + 1) * 2 * Q)
        if in_two_hops(chunk):
            for way, ref in enumerate((gb_ref, gc_ref)):
                total = paired(chunk, chip, way) + hop1_in[chunk, way, 0]
                hop_copy(chunk, 1, way).wait_recv()
                ref[:, at] = total + hop2_in[chunk, way]
        else:
            total = send2[chunk, chip]
            for d in range(1, chips):
                chip_copy(chunk, d).wait_recv()
                total = total + recv2[chunk, d - 1]
            gb_ref[:, at] = total[:each]
            gc_ref[:, at] = total[each:]

    def sent(chunk):
        pair_copy(chunk).wait_send()
        if in_two_hops(chunk):
            for way in range(2):
                hop_copy(chunk, 0, way).wait_send()
                hop_copy(chunk, 1, way).wait_send()
        else:
            for d in range(1, chips):
                chip_copy(chunk, d).wait_send()

    for k in range(blocks):
        intra_w(k)
    ctx_wait(0)
    for r in range(1, hops):
        out_s[r] = out_s[0] + decay_dev * in_s[r - 1]
        out_g[r] = out_g[0] + decay_dev * in_g[r - 1]
        ctx_start(r, 0)
        ctx_start(r, 1)
        ctx_wait(r)
    state_in = in_s[hops - 1]
    grad_in = in_g[hops - 1]
    for k in range(blocks):
        inter_w(k, state_in, grad_in)
        if fused and k % 2 == 1:
            pair_copy(k // 2).start()
    for k in range(blocks):
        if fused and k < blocks // 2:
            second(k)
        outer(k, state_in)

    q8 = jnp.concatenate(qs, axis=0)
    r8 = jnp.concatenate(diffs, axis=0)
    tail8 = jnp.concatenate(tails, axis=0)
    back8 = lax.dot_general(
        r8, lower_ones, (((1,), (0,)), ((), ())), precision=HIGH, preferred_element_type=F32
    )
    gdt8 = q8 / dt8 - rate * (back8 + tail8)
    for k in range(blocks):
        gdt_ref[0:1, k * Q : (k + 1) * Q] = gdt8[k : k + 1]

    for r in range(hops):
        ctx_done(r)
    if fused:
        for chunk in range(blocks // 2):
            if in_two_hops(chunk):
                third(chunk)
        for chunk in range(blocks // 2):
            last(chunk)
        for chunk in range(blocks // 2):
            sent(chunk)


def move(*refs):
    count = (len(refs) - 1) // 2
    sem = refs[-1]
    copies = [pltpu.make_async_copy(refs[i], refs[count + i], sem.at[i]) for i in range(count)]
    for copy in copies:
        copy.start()
    for copy in copies:
        copy.wait()


def per_device(n_ctx, n_head, inputs, dt, decay_rate, skip, b_proj, c_proj, lengths, grad_out):
    _, width_p, local = inputs.shape
    width_n = b_proj.shape[0]
    longest = n_ctx * local // 4
    hops = max(1, min(n_ctx - 1, (longest - 2) // local + 1))
    each = width_n // n_head
    fused = each % 8 == 0
    blocks = local // Q
    chips = n_head // 2
    chunks = blocks // 2
    vmem = pl.BlockSpec(memory_space=pltpu.VMEM)
    smem = pl.BlockSpec(memory_space=pltpu.SMEM)
    anywhere = pl.BlockSpec(memory_space=pl.ANY)
    result = pltpu.VMEM if fused else jax.ShapeDtypeStruct
    grad_rows = each if fused else width_n
    scratch = [
        pltpu.SMEM(lengths.shape, lengths.dtype),
        pltpu.VMEM(inputs.shape, BF16),
        pltpu.VMEM(dt.shape, F32),
        pltpu.VMEM(b_proj.shape, BF16),
        pltpu.VMEM(c_proj.shape, BF16),
        pltpu.VMEM(grad_out.shape, BF16),
        pltpu.SemaphoreType.DMA((6,)),
        pltpu.VMEM((blocks, width_p, width_n), F32),
        pltpu.VMEM((blocks, width_p, width_n), F32),
        pltpu.VMEM((blocks, Q, Q), F32),
        pltpu.VMEM((hops, width_p, width_n), F32),
        pltpu.VMEM((hops, width_p, width_n), F32),
        pltpu.VMEM((hops, width_p, width_n), F32),
        pltpu.VMEM((hops, width_p, width_n), F32),
        pltpu.SemaphoreType.DMA((hops, 2)),
        pltpu.SemaphoreType.DMA((hops, 2)),
    ]
    if fused:
        scratch += [
            pltpu.VMEM((chunks, 2, chips, 2 * each, 2 * Q), F32),
            pltpu.VMEM((chunks, chips, 2 * each, 2 * Q), F32),
            pltpu.VMEM((chunks, chips, 2 * each, 2 * Q), F32),
            pltpu.VMEM((chunks, chips - 1, 2 * each, 2 * Q), F32),
            pltpu.VMEM((chunks, 2, 2, each, 2 * Q), F32),
            pltpu.VMEM((chunks, 2, 2, each, 2 * Q), F32),
            pltpu.VMEM((chunks, 2, each, 2 * Q), F32),
            pltpu.VMEM((chunks, 2, each, 2 * Q), F32),
            pltpu.SemaphoreType.DMA((chunks,)),
            pltpu.SemaphoreType.DMA((chunks,)),
            pltpu.SemaphoreType.DMA((chunks, max(4, chips - 1))),
            pltpu.SemaphoreType.DMA((chunks, max(4, chips - 1))),
        ]
    mixed, gx, gdt, gb, gc = pl.pallas_call(
        functools.partial(kernel, (n_ctx, n_head, hops, fused, lengths.shape[0])),
        out_shape=(
            result(inputs.shape, BF16),
            result(inputs.shape, BF16),
            result(dt.shape, F32),
            result((grad_rows, local), F32),
            result((grad_rows, local), F32),
        ),
        in_specs=[smem, smem] + [anywhere] * 6,
        out_specs=(vmem,) * 5,
        scratch_shapes=scratch,
        compiler_params=pltpu.CompilerParams(collective_id=0, has_side_effects=True),
    )(decay_rate, skip, lengths, inputs, dt, b_proj, c_proj, grad_out)
    if not fused:
        gb = lax.psum_scatter(gb, "head", scatter_dimension=0, tiled=True)
        gc = lax.psum_scatter(gc, "head", scatter_dimension=0, tiled=True)
    results = (mixed, gx, gdt, gb, gc)
    if fused:
        results = tuple(pltpu.with_memory_space_constraint(r, pltpu.VMEM) for r in results)
    return pl.pallas_call(
        move,
        out_shape=tuple(jax.ShapeDtypeStruct(r.shape, r.dtype) for r in results),
        in_specs=[vmem if fused else anywhere] * 5,
        out_specs=(anywhere,) * 5,
        scratch_shapes=[pltpu.SemaphoreType.DMA((5,))],
    )(*results)


def solution(mesh):
    return jax.shard_map(
        functools.partial(per_device, mesh.shape["ctx"], mesh.shape["head"]),
        mesh=mesh,
        in_specs=(
            P("head", None, "ctx"),
            P("head", "ctx"),
            P("head"),
            P("head"),
            P(None, "ctx"),
            P(None, "ctx"),
            P(),
            P("head", None, "ctx"),
        ),
        out_specs=(
            P("head", None, "ctx"),
            P("head", None, "ctx"),
            P("head", "ctx"),
            P("head", "ctx"),
            P("head", "ctx"),
        ),
        check_vma=False,
    )
```

```python
import functools
import jax
import jax.numpy as jnp
from jax import lax
from jax.experimental import pallas as pl
from jax.experimental.pallas import tpu as pltpu
from jax.sharding import PartitionSpec as P

Q = 128
DIRECT = 2
HIGH = lax.Precision.HIGHEST
F32 = jnp.float32
BF16 = jnp.bfloat16
MESH = pl.DeviceIdType.MESH


def mm(a, b, ca, cb):
    return lax.dot_general(a, b, (((ca,), (cb,)), ((), ())), preferred_element_type=F32)


def split(v):
    hi = v.astype(BF16)
    return hi, (v - hi.astype(F32)).astype(BF16)


def lanes(a, b):
    return jnp.concatenate([a, b], axis=1)


def rows(a, b):
    return jnp.concatenate([a, b], axis=0)


def kernel(cfg, rate_ref, skip_ref, len_in, x_in, dt_in, b_in, c_in, g_in, *refs):
    n_ctx, n_head, hops, fused, ndoc = cfg
    mixed_ref, gx_ref, gdt_ref, gb_ref, gc_ref = refs[:5]
    len_ref, x_ref, dt_ref, b_ref, c_ref, g_ref, load_sem = refs[5:12]
    (s_ref, gz_ref, ddt_ref, out_s, out_g, in_s, in_g, ctx_send, ctx_recv) = refs[12:21]
    scaled, halves = refs[21:23]
    if fused:
        part, recv1, send2, recv2, hop1_out, hop1_in, hop2_out, hop2_in = refs[23:31]
        s1_send, s1_recv, s2_send, s2_recv = refs[31:35]
        other_scaled, other_in, other_send, other_recv = refs[35:]
    width_p = x_ref.shape[1]
    local = x_ref.shape[2]
    width_n = b_ref.shape[0]
    blocks = local // Q
    each = width_n // n_head
    me = lax.axis_index("ctx")
    head = lax.axis_index("head")
    chips = n_head // 2
    core = lax.rem(head, 2)
    chip = head // 2

    barrier = pltpu.get_barrier_semaphore()

    def beside(step, cross):
        to = {"ctx": me + step}
        if cross:
            to["head"] = chip * 2 + 1 - core
        return to

    for cross in range(2 if fused else 1):

        @pl.when(me > 0)
        def _():
            pl.semaphore_signal(barrier, inc=1, device_id=beside(-1, cross), device_id_type=MESH)

        @pl.when(me < n_ctx - 1)
        def _():
            pl.semaphore_signal(barrier, inc=1, device_id=beside(1, cross), device_id_type=MESH)

    if fused:
        pl.semaphore_signal(
            barrier, inc=1, device_id={"head": chip * 2 + 1 - core}, device_id_type=MESH
        )
        for d in range(1, chips):
            to = lax.rem(chip + d, chips) * 2 + core
            pl.semaphore_signal(barrier, inc=1, device_id={"head": to}, device_id_type=MESH)

    pairs = (
        (len_in, len_ref),
        (dt_in, dt_ref),
        (x_in, x_ref),
        (b_in, b_ref),
        (g_in, g_ref),
        (c_in, c_ref),
    )
    loads = [
        pltpu.make_async_copy(src, dst, load_sem.at[i]) for i, (src, dst) in enumerate(pairs)
    ]
    for load in loads:
        load.start()
    len_load, dt_load, x_load, b_load, g_load, c_load = loads

    rate = rate_ref[0]
    skip = skip_ref[0]
    offset = me * local

    len_load.wait()
    ends = []
    total = len_ref[0]
    for j in range(ndoc - 1):
        ends.append(total)
        total = total + len_ref[j + 1]

    def segment_of(pos):
        seg = jnp.zeros(pos.shape, jnp.int32)
        for end in ends:
            seg = seg + (pos >= end).astype(jnp.int32)
        return seg

    pos8 = (
        offset
        + lax.broadcasted_iota(jnp.int32, (blocks, Q), 0) * Q
        + lax.broadcasted_iota(jnp.int32, (blocks, Q), 1)
    )
    pos_t = (
        offset
        + lax.broadcasted_iota(jnp.int32, (Q, blocks), 1) * Q
        + lax.broadcasted_iota(jnp.int32, (Q, blocks), 0)
    )
    seg8 = segment_of(pos8)
    seg_t = segment_of(pos_t)
    before8 = jnp.where(pos8 == 0, -1, segment_of(pos8 - 1))
    prev8 = before8[:, 0:1]
    last8 = seg8[:, Q - 1 : Q]

    dt_load.wait()
    dt8 = jnp.concatenate([dt_ref[0:1, k * Q : (k + 1) * Q] for k in range(blocks)], axis=0)
    row_i = lax.broadcasted_iota(jnp.int32, (Q, Q), 0)
    col_j = lax.broadcasted_iota(jnp.int32, (Q, Q), 1)
    lower = row_i >= col_j
    lower_ones = lower.astype(F32)
    log8 = -rate * dt8
    cum8 = lax.dot_general(
        log8, lower_ones, (((1,), (1,)), ((), ())), precision=HIGH, preferred_element_type=F32
    )
    cum_t = lax.dot_general(
        lower_ones, log8, (((1,), (1,)), ((), ())), precision=HIGH, preferred_element_type=F32
    )
    end8 = cum8[:, Q - 1 : Q]
    din8 = jnp.where(seg8 == prev8, jnp.exp(cum8), 0.0)
    wdt8 = jnp.where(seg8 == last8, jnp.exp(end8 - cum8), 0.0) * dt8
    dall8 = jnp.where(last8 == prev8, jnp.exp(end8), 0.0)

    def cut(ref, k):
        return ref[0, :, k * Q : (k + 1) * Q]

    def cut2(ref, k):
        return ref[:, k * Q : (k + 1) * Q]

    ahead = [None] * blocks
    prod = jnp.ones((1, 1), F32)
    for k in range(blocks):
        ahead[k] = prod
        prod = prod * dall8[k : k + 1]
    decay_dev = prod
    behind = [None] * blocks
    prod = jnp.ones((1, 1), F32)
    for k in reversed(range(blocks)):
        behind[k] = prod
        prod = prod * dall8[k : k + 1]

    @pl.when(me == 0)
    def _():
        in_s[...] = jnp.zeros_like(in_s)
        if fused:
            other_in[1] = jnp.zeros((width_p, width_n), F32)

    @pl.when(me == n_ctx - 1)
    def _():
        in_g[...] = jnp.zeros_like(in_g)
        if fused:
            other_in[0] = jnp.zeros((width_p, width_n), F32)

    peers = chips if fused else 0
    at_end = (me == 0) | (me == n_ctx - 1)

    def meet():
        @pl.when(at_end)
        def _():
            pl.semaphore_wait(barrier, peers + (2 if fused else 1))

        @pl.when(jnp.logical_not(at_end))
        def _():
            pl.semaphore_wait(barrier, peers + (4 if fused else 2))

    def ctx_copy(r, way):
        src, dst = (out_s, in_s) if way == 0 else (out_g, in_g)
        return pltpu.make_async_remote_copy(
            src_ref=src.at[r],
            dst_ref=dst.at[r],
            send_sem=ctx_send.at[r, way],
            recv_sem=ctx_recv.at[r, way],
            device_id={"ctx": me + 1 if way == 0 else me - 1},
            device_id_type=MESH,
        )

    def cross_copy(way):
        return pltpu.make_async_remote_copy(
            src_ref=(out_g, out_s)[way].at[hops - 1],
            dst_ref=other_in.at[way],
            send_sem=other_send.at[way],
            recv_sem=other_recv.at[way],
            device_id=beside((-1, 1)[way], 1),
            device_id_type=MESH,
        )

    def ctx_start(r, way):
        @pl.when(me < n_ctx - 1 if way == 0 else me > 0)
        def _():
            ctx_copy(r, way).start()
            if fused and r == hops - 1:
                cross_copy(1 - way).start()

    def ctx_wait(r):
        @pl.when(me > 0)
        def _():
            ctx_copy(r, 0).wait_recv()
            if fused and r == hops - 1:
                cross_copy(1).wait_recv()

        @pl.when(me < n_ctx - 1)
        def _():
            ctx_copy(r, 1).wait_recv()
            if fused and r == hops - 1:
                cross_copy(0).wait_recv()

    def ctx_done(r):
        @pl.when(me < n_ctx - 1)
        def _():
            ctx_copy(r, 0).wait_send()
            if fused and r == hops - 1:
                cross_copy(1).wait_send()

        @pl.when(me > 0)
        def _():
            ctx_copy(r, 1).wait_send()
            if fused and r == hops - 1:
                cross_copy(0).wait_send()

    def scaled_copy(way):
        return pltpu.make_async_remote_copy(
            src_ref=scaled.at[way],
            dst_ref=other_scaled.at[way],
            send_sem=other_send.at[2 + way],
            recv_sem=other_recv.at[2 + way],
            device_id={"head": chip * 2 + 1 - core},
            device_id_type=MESH,
        )

    x_load.wait()
    b_load.wait()
    state = jnp.zeros((width_p, width_n), F32)
    for k in range(blocks):
        s_ref[k] = state
        b_k = cut2(b_ref, k)
        hi, lo = split(cut(x_ref, k).astype(F32) * wdt8[k : k + 1])
        state = dall8[k : k + 1] * state + mm(lanes(hi, lo), lanes(b_k, b_k), 1, 1)
    out_s[0] = state
    meet()
    ctx_start(0, 0)
    g_load.wait()
    c_load.wait()
    carry = jnp.zeros((width_p, width_n), F32)
    for k in reversed(range(blocks)):
        gz_ref[k] = carry
        c_k = cut2(c_ref, k)
        hi, lo = split(cut(g_ref, k).astype(F32) * din8[k : k + 1])
        carry = dall8[k : k + 1] * carry + mm(lanes(hi, lo), lanes(c_k, c_k), 1, 1)
    out_g[0] = carry
    ctx_start(0, 1)

    def put(k, way, value):
        if fused:
            chunk, lo = k // 2, (k % 2) * Q
            for h in range(n_head):
                at = (chunk, h % 2, h // 2, slice(way * each, (way + 1) * each), slice(lo, lo + Q))
                part[at] = value[h * each : (h + 1) * each]
        else:
            ref = (gb_ref, gc_ref)[way]
            ref[:, k * Q : (k + 1) * Q] = value

    def scale(k):
        at = slice(k * Q, (k + 1) * Q)
        scaled[0, :, at] = cut(x_ref, k).astype(F32) * (wdt8[k : k + 1] * behind[k])
        scaled[1, :, at] = cut(g_ref, k).astype(F32) * (din8[k : k + 1] * ahead[k])

    def local_w(k):
        x_k, g_k, b_k, c_k = cut(x_ref, k), cut(g_ref, k), cut2(b_ref, k), cut2(c_ref, k)
        mask = lower & (seg_t[:, k : k + 1] == seg8[k : k + 1])
        gap = jnp.where(mask, cum_t[:, k : k + 1] - cum8[k : k + 1], 0.0)
        ddt = jnp.where(mask, jnp.exp(gap), 0.0) * dt8[k : k + 1]
        ddt_ref[k] = ddt
        w_hi, w_lo = split(mm(g_k, x_k, 0, 0) * ddt)
        grad_b = mm(lanes(c_k, c_k), rows(w_hi, w_lo), 1, 0)
        grad_c = mm(lanes(b_k, b_k), lanes(w_hi, w_lo), 1, 1)
        if k < blocks - 1:
            z_hi, z_lo = split(gz_ref[k])
            grad_b += mm(rows(z_hi, z_lo), rows(x_k, x_k), 0, 0) * wdt8[k : k + 1]
        if k > 0:
            s_hi, s_lo = split(s_ref[k])
            grad_c += mm(rows(s_hi, s_lo), rows(g_k, g_k), 0, 0) * din8[k : k + 1]
        put(k, 0, grad_b)
        put(k, 1, grad_c)

    diffs, qs, tails = [None] * blocks, [None] * blocks, [None] * blocks

    def halve(way):
        both = scaled[way]
        if fused:
            both = rows(both, other_scaled[way])
        hi, lo = split(both)
        halves[way, 0] = hi
        halves[way, 1] = lo

    def turned(way):
        both = (in_g, in_s)[way][hops - 1]
        if fused:
            both = rows(both, other_in[way]).T
            both = jnp.concatenate(
                [
                    jnp.where(
                        core == 0,
                        both[2 * h * each : (2 * h + 1) * each],
                        both[(2 * h + 1) * each : (2 * h + 2) * each],
                    )
                    for h in range(chips)
                ],
                axis=0,
            )
        else:
            both = both.T
        hi, lo = split(both)
        return jnp.concatenate([hi, hi, lo], axis=1)

    def remote(chunk, way):
        at = slice(chunk * 2 * Q, (chunk + 1) * 2 * Q)
        hi, lo = halves[way, 0, :, at], halves[way, 1, :, at]
        return mm(states[way], jnp.concatenate([hi, lo, hi], axis=0), 1, 0)

    def outer(k, state_in, grad_in):
        x_k, g_k, b_k, c_k = cut(x_ref, k), cut(g_ref, k), cut2(b_ref, k), cut2(c_ref, k)
        s_k = s_ref[k] + ahead[k] * state_in
        gz = gz_ref[k] + behind[k] * grad_in
        if k + 1 < blocks:
            s_end = s_ref[k + 1] + ahead[k + 1] * state_in
        else:
            s_end = out_s[0] + decay_dev * state_in
        tails[k] = jnp.sum(jnp.sum(gz * s_end, axis=0, keepdims=True), axis=1, keepdims=True)
        a_hi, a_lo = split(mm(c_k, b_k, 0, 0) * ddt_ref[k])
        s_hi, s_lo = split(s_k)
        z_hi, z_lo = split(gz)
        din, wdt = din8[k : k + 1], wdt8[k : k + 1]
        y = mm(lanes(x_k, x_k), lanes(a_hi, a_lo), 1, 1)
        y = y + mm(lanes(s_hi, s_lo), rows(c_k, c_k), 1, 0) * din
        v = mm(lanes(g_k, g_k), rows(a_hi, a_lo), 1, 0)
        v = v + mm(lanes(z_hi, z_lo), rows(b_k, b_k), 1, 0) * wdt
        x_f, g_f = x_k.astype(F32), g_k.astype(F32)
        mixed_ref[0, :, k * Q : (k + 1) * Q] = (y + skip * x_f).astype(BF16)
        gx_ref[0, :, k * Q : (k + 1) * Q] = (v + skip * g_f).astype(BF16)
        q_k = jnp.sum(x_f * v, axis=0, keepdims=True)
        qs[k] = q_k
        diffs[k] = jnp.sum(g_f * y, axis=0, keepdims=True) - q_k

    def pair_copy(chunk):
        return pltpu.make_async_remote_copy(
            src_ref=part.at[chunk, 1 - core],
            dst_ref=recv1.at[chunk],
            send_sem=s1_send.at[chunk],
            recv_sem=s1_recv.at[chunk],
            device_id={"head": chip * 2 + 1 - core},
            device_id_type=MESH,
        )

    def chip_copy(chunk, d):
        to = lax.rem(chip + d, chips)
        return pltpu.make_async_remote_copy(
            src_ref=send2.at[chunk, to],
            dst_ref=recv2.at[chunk, d - 1],
            send_sem=s2_send.at[chunk, d - 1],
            recv_sem=s2_recv.at[chunk, d - 1],
            device_id={"head": to * 2 + core},
            device_id_type=MESH,
        )

    def hop_copy(chunk, hop, way):
        src, dst = (hop1_out, hop1_in) if hop == 0 else (hop2_out, hop2_in)
        to = chip ^ (1 + (way + hop) % 2)
        return pltpu.make_async_remote_copy(
            src_ref=src.at[chunk, way],
            dst_ref=dst.at[chunk, way],
            send_sem=s2_send.at[chunk, 2 * hop + way],
            recv_sem=s2_recv.at[chunk, 2 * hop + way],
            device_id={"head": to * 2 + core},
            device_id_type=MESH,
        )

    def paired(chunk, to, way):
        return send2[chunk, to, way * each : (way + 1) * each]

    def in_two_hops(chunk):
        return chips == 4 and chunk < blocks // 2 - DIRECT

    def second(chunk):
        pair_copy(chunk).wait_recv()
        for way in range(2):
            far = remote(chunk, way)
            for h in range(chips):
                at = (h, slice(way * each, (way + 1) * each))
                near = part[(chunk, core) + at] + recv1[(chunk,) + at]
                send2[(chunk,) + at] = near + far[h * each : (h + 1) * each]
        if in_two_hops(chunk):
            for way in range(2):
                hop1_out[chunk, way, 0] = paired(chunk, chip ^ (1 + way), way)
                hop1_out[chunk, way, 1] = paired(chunk, chip ^ 3, way)
                hop_copy(chunk, 0, way).start()
        else:
            for d in range(1, chips):
                chip_copy(chunk, d).start()

    def third(chunk):
        for way in range(2):
            hop_copy(chunk, 0, way).wait_recv()
            hop2_out[chunk, way] = paired(chunk, chip ^ (2 - way), way) + hop1_in[chunk, way, 1]
            hop_copy(chunk, 1, way).start()

    def last(chunk):
        at = slice(chunk * 2 * Q, (chunk + 1) * 2 * Q)
        if in_two_hops(chunk):
            for way, ref in enumerate((gb_ref, gc_ref)):
                total = paired(chunk, chip, way) + hop1_in[chunk, way, 0]
                hop_copy(chunk, 1, way).wait_recv()
                ref[:, at] = total + hop2_in[chunk, way]
        else:
            total = send2[chunk, chip]
            for d in range(1, chips):
                chip_copy(chunk, d).wait_recv()
                total = total + recv2[chunk, d - 1]
            gb_ref[:, at] = total[:each]
            gc_ref[:, at] = total[each:]

    def sent(chunk):
        pair_copy(chunk).wait_send()
        if in_two_hops(chunk):
            for way in range(2):
                hop_copy(chunk, 0, way).wait_send()
                hop_copy(chunk, 1, way).wait_send()
        else:
            for d in range(1, chips):
                chip_copy(chunk, d).wait_send()

    for k in range(blocks):
        scale(k)
    if fused:
        scaled_copy(0).start()
        scaled_copy(1).start()
    for k in range(blocks):
        local_w(k)
        if fused and k % 2 == 1:
            pair_copy(k // 2).start()
    for way in range(2):
        if fused:
            scaled_copy(way).wait_recv()
        halve(way)
    ctx_wait(0)
    for r in range(1, hops):
        out_s[r] = out_s[0] + decay_dev * in_s[r - 1]
        out_g[r] = out_g[0] + decay_dev * in_g[r - 1]
        ctx_start(r, 0)
        ctx_start(r, 1)
        ctx_wait(r)
    state_in = in_s[hops - 1]
    grad_in = in_g[hops - 1]
    states = [turned(way) for way in range(2)]
    for chunk in range(blocks // 2):
        if fused:
            second(chunk)
        else:
            for way, ref in enumerate((gb_ref, gc_ref)):
                at = slice(chunk * 2 * Q, (chunk + 1) * 2 * Q)
                ref[:, at] = ref[:, at] + remote(chunk, way)
    for k in range(blocks):
        outer(k, state_in, grad_in)

    q8 = jnp.concatenate(qs, axis=0)
    r8 = jnp.concatenate(diffs, axis=0)
    tail8 = jnp.concatenate(tails, axis=0)
    back8 = lax.dot_general(
        r8, lower_ones, (((1,), (0,)), ((), ())), precision=HIGH, preferred_element_type=F32
    )
    gdt8 = q8 / dt8 - rate * (back8 + tail8)
    for k in range(blocks):
        gdt_ref[0:1, k * Q : (k + 1) * Q] = gdt8[k : k + 1]

    for r in range(hops):
        ctx_done(r)
    if fused:
        for chunk in range(blocks // 2):
            if in_two_hops(chunk):
                third(chunk)
        for chunk in range(blocks // 2):
            last(chunk)
        for chunk in range(blocks // 2):
            sent(chunk)
        for way in range(2):
            scaled_copy(way).wait_send()


def move(*refs):
    count = (len(refs) - 1) // 2
    sem = refs[-1]
    copies = [pltpu.make_async_copy(refs[i], refs[count + i], sem.at[i]) for i in range(count)]
    for copy in copies:
        copy.start()
    for copy in copies:
        copy.wait()


def per_device(n_ctx, n_head, inputs, dt, decay_rate, skip, b_proj, c_proj, lengths, grad_out):
    _, width_p, local = inputs.shape
    width_n = b_proj.shape[0]
    longest = n_ctx * local // 4
    hops = max(1, min(n_ctx - 1, (longest - 2) // local + 1))
    each = width_n // n_head
    fused = each % 8 == 0
    blocks = local // Q
    chips = n_head // 2
    chunks = blocks // 2
    vmem = pl.BlockSpec(memory_space=pltpu.VMEM)
    smem = pl.BlockSpec(memory_space=pltpu.SMEM)
    anywhere = pl.BlockSpec(memory_space=pl.ANY)
    result = pltpu.VMEM if fused else jax.ShapeDtypeStruct
    grad_rows = each if fused else width_n
    scratch = [
        pltpu.SMEM(lengths.shape, lengths.dtype),
        pltpu.VMEM(inputs.shape, BF16),
        pltpu.VMEM(dt.shape, F32),
        pltpu.VMEM(b_proj.shape, BF16),
        pltpu.VMEM(c_proj.shape, BF16),
        pltpu.VMEM(grad_out.shape, BF16),
        pltpu.SemaphoreType.DMA((6,)),
        pltpu.VMEM((blocks, width_p, width_n), F32),
        pltpu.VMEM((blocks, width_p, width_n), F32),
        pltpu.VMEM((blocks, Q, Q), F32),
        pltpu.VMEM((hops, width_p, width_n), F32),
        pltpu.VMEM((hops, width_p, width_n), F32),
        pltpu.VMEM((hops, width_p, width_n), F32),
        pltpu.VMEM((hops, width_p, width_n), F32),
        pltpu.SemaphoreType.DMA((hops, 2)),
        pltpu.SemaphoreType.DMA((hops, 2)),
        pltpu.VMEM((2, width_p, local), F32),
        pltpu.VMEM((2, 2, (2 if fused else 1) * width_p, local), BF16),
    ]
    if fused:
        scratch += [
            pltpu.VMEM((chunks, 2, chips, 2 * each, 2 * Q), F32),
            pltpu.VMEM((chunks, chips, 2 * each, 2 * Q), F32),
            pltpu.VMEM((chunks, chips, 2 * each, 2 * Q), F32),
            pltpu.VMEM((chunks, chips - 1, 2 * each, 2 * Q), F32),
            pltpu.VMEM((chunks, 2, 2, each, 2 * Q), F32),
            pltpu.VMEM((chunks, 2, 2, each, 2 * Q), F32),
            pltpu.VMEM((chunks, 2, each, 2 * Q), F32),
            pltpu.VMEM((chunks, 2, each, 2 * Q), F32),
            pltpu.SemaphoreType.DMA((chunks,)),
            pltpu.SemaphoreType.DMA((chunks,)),
            pltpu.SemaphoreType.DMA((chunks, max(4, chips - 1))),
            pltpu.SemaphoreType.DMA((chunks, max(4, chips - 1))),
            pltpu.VMEM((2, width_p, local), F32),
            pltpu.VMEM((2, width_p, width_n), F32),
            pltpu.SemaphoreType.DMA((4,)),
            pltpu.SemaphoreType.DMA((4,)),
        ]
    mixed, gx, gdt, gb, gc = pl.pallas_call(
        functools.partial(kernel, (n_ctx, n_head, hops, fused, lengths.shape[0])),
        out_shape=(
            result(inputs.shape, BF16),
            result(inputs.shape, BF16),
            result(dt.shape, F32),
            result((grad_rows, local), F32),
            result((grad_rows, local), F32),
        ),
        in_specs=[smem, smem] + [anywhere] * 6,
        out_specs=(vmem,) * 5,
        scratch_shapes=scratch,
        compiler_params=pltpu.CompilerParams(collective_id=0, has_side_effects=True),
    )(decay_rate, skip, lengths, inputs, dt, b_proj, c_proj, grad_out)
    if not fused:
        gb = lax.psum_scatter(gb, "head", scatter_dimension=0, tiled=True)
        gc = lax.psum_scatter(gc, "head", scatter_dimension=0, tiled=True)
    results = (mixed, gx, gdt, gb, gc)
    if fused:
        results = tuple(pltpu.with_memory_space_constraint(r, pltpu.VMEM) for r in results)
    return pl.pallas_call(
        move,
        out_shape=tuple(jax.ShapeDtypeStruct(r.shape, r.dtype) for r in results),
        in_specs=[vmem if fused else anywhere] * 5,
        out_specs=(anywhere,) * 5,
        scratch_shapes=[pltpu.SemaphoreType.DMA((5,))],
    )(*results)


def solution(mesh):
    return jax.shard_map(
        functools.partial(per_device, mesh.shape["ctx"], mesh.shape["head"]),
        mesh=mesh,
        in_specs=(
            P("head", None, "ctx"),
            P("head", "ctx"),
            P("head"),
            P("head"),
            P(None, "ctx"),
            P(None, "ctx"),
            P(),
            P("head", None, "ctx"),
        ),
        out_specs=(
            P("head", None, "ctx"),
            P("head", None, "ctx"),
            P("head", "ctx"),
            P("head", "ctx"),
            P("head", "ctx"),
        ),
        check_vma=False,
    )
```

```python
import functools
import jax
import jax.numpy as jnp
from jax import lax
from jax.experimental import pallas as pl
from jax.experimental.pallas import tpu as pltpu
from jax.sharding import PartitionSpec as P

Q = 128
EARLY = 2
STRAIGHT = 1
TURN = (1, 3, 7, 7)
HIGH = lax.Precision.HIGHEST
F32 = jnp.float32
BF16 = jnp.bfloat16
MESH = pl.DeviceIdType.MESH


def mm(a, b, ca, cb):
    return lax.dot_general(a, b, (((ca,), (cb,)), ((), ())), preferred_element_type=F32)


def split(v):
    hi = v.astype(BF16)
    return hi, (v - hi.astype(F32)).astype(BF16)


def lanes(*parts):
    return jnp.concatenate(parts, axis=1)


def rows(*parts):
    return jnp.concatenate(parts, axis=0)


def kernel(cfg, rate_ref, skip_ref, len_in, x_in, dt_in, b_in, c_in, g_in, *refs):
    n_ctx, n_head, hops, fused, ndoc, hopping, early = cfg
    mixed_ref, gx_ref, gdt_ref, gb_ref, gc_ref = refs[:5]
    len_ref, x_ref, dt_ref, b_ref, c_ref, g_ref, load_sem = refs[5:12]
    (s_ref, gz_ref, ddt_ref, out_s, out_g, in_s, in_g, ctx_send, ctx_recv) = refs[12:21]
    if fused:
        part, pair_in, near, hop1_out, hop1_in, hop2_out, hop2_in, chip_in = refs[21:29]
        far, far_in, scaled, other_scaled, halves = refs[29:34]
        pair_send, pair_recv, hop_send, hop_recv, chip_send, chip_recv, far_sem, scaled_sem = refs[34:]
    width_p = x_ref.shape[1]
    local = x_ref.shape[2]
    width_n = b_ref.shape[0]
    blocks = local // Q
    chunks = blocks // 2
    each = width_n // n_head
    me = lax.axis_index("ctx")
    head = lax.axis_index("head")
    chips = n_head // 2
    core = lax.rem(head, 2)
    chip = head // 2
    mate = {"head": chip * 2 + 1 - core}

    barrier = pltpu.get_barrier_semaphore()

    def beside(step, cross):
        to = {"ctx": me + step}
        if cross:
            to.update(mate)
        return to

    for cross in range(2 if fused else 1):

        @pl.when(me > 0)
        def _():
            pl.semaphore_signal(barrier, inc=1, device_id=beside(-1, cross), device_id_type=MESH)

        @pl.when(me < n_ctx - 1)
        def _():
            pl.semaphore_signal(barrier, inc=1, device_id=beside(1, cross), device_id_type=MESH)

    if fused:
        pl.semaphore_signal(barrier, inc=1, device_id=mate, device_id_type=MESH)
        for d in range(1, chips):
            to = lax.rem(chip + d, chips) * 2 + core
            pl.semaphore_signal(barrier, inc=1, device_id={"head": to}, device_id_type=MESH)

    pairs = (
        (dt_in, dt_ref),
        (len_in, len_ref),
        (x_in, x_ref),
        (b_in, b_ref),
        (g_in, g_ref),
        (c_in, c_ref),
    )
    loads = [
        pltpu.make_async_copy(src, dst, load_sem.at[i]) for i, (src, dst) in enumerate(pairs)
    ]
    for load in loads:
        load.start()

    rate = rate_ref[0]
    skip = skip_ref[0]
    offset = me * local

    row_i = lax.broadcasted_iota(jnp.int32, (Q, Q), 0)
    col_j = lax.broadcasted_iota(jnp.int32, (Q, Q), 1)
    lower = row_i >= col_j
    lower_ones = lower.astype(F32)
    loads[0].wait()
    dt8 = rows(*[dt_ref[0:1, k * Q : (k + 1) * Q] for k in range(blocks)])
    log8 = -rate * dt8
    cum8 = lax.dot_general(
        log8, lower_ones, (((1,), (1,)), ((), ())), precision=HIGH, preferred_element_type=F32
    )
    cum_t = lax.dot_general(
        lower_ones, log8, (((1,), (1,)), ((), ())), precision=HIGH, preferred_element_type=F32
    )
    end8 = cum8[:, Q - 1 : Q]

    loads[1].wait()
    ends = []
    total = len_ref[0]
    for j in range(ndoc - 1):
        ends.append(total)
        total = total + len_ref[j + 1]

    def segment_of(pos):
        seg = jnp.zeros(pos.shape, jnp.int32)
        for end in ends:
            seg = seg + (pos >= end).astype(jnp.int32)
        return seg

    pos8 = (
        offset
        + lax.broadcasted_iota(jnp.int32, (blocks, Q), 0) * Q
        + lax.broadcasted_iota(jnp.int32, (blocks, Q), 1)
    )
    pos_t = (
        offset
        + lax.broadcasted_iota(jnp.int32, (Q, blocks), 1) * Q
        + lax.broadcasted_iota(jnp.int32, (Q, blocks), 0)
    )
    seg8 = segment_of(pos8)
    seg_t = segment_of(pos_t)
    before8 = jnp.where(pos8 == 0, -1, segment_of(pos8 - 1))
    prev8 = before8[:, 0:1]
    last8 = seg8[:, Q - 1 : Q]
    first8 = seg8 == before8[0:1, 0:1]

    din8 = jnp.where(seg8 == prev8, jnp.exp(cum8), 0.0)
    wdt8 = jnp.where(seg8 == last8, jnp.exp(end8 - cum8), 0.0) * dt8
    dall8 = jnp.where(last8 == prev8, jnp.exp(end8), 0.0)

    def cut(ref, k):
        return ref[0, :, k * Q : (k + 1) * Q]

    def cut2(ref, k):
        return ref[:, k * Q : (k + 1) * Q]

    ahead = [None] * blocks
    prod = jnp.ones((1, 1), F32)
    for k in range(blocks):
        ahead[k] = prod
        prod = prod * dall8[k : k + 1]
    decay_dev = prod
    behind = [None] * blocks
    prod = jnp.ones((1, 1), F32)
    for k in reversed(range(blocks)):
        behind[k] = prod
        prod = prod * dall8[k : k + 1]

    @pl.when(me == 0)
    def _():
        in_s[...] = jnp.zeros_like(in_s)

    @pl.when(me == n_ctx - 1)
    def _():
        in_g[...] = jnp.zeros_like(in_g)

    at_end = (me == 0) | (me == n_ctx - 1)
    peers = chips if fused else 0
    beside_count = 2 if fused else 1

    def meet():
        @pl.when(at_end)
        def _():
            pl.semaphore_wait(barrier, peers + beside_count)

        @pl.when(jnp.logical_not(at_end))
        def _():
            pl.semaphore_wait(barrier, peers + 2 * beside_count)

    def ctx_copy(r, way, cross):
        src, dst = (out_s, in_s) if way == 0 else (out_g, in_g)
        return pltpu.make_async_remote_copy(
            src_ref=src.at[r],
            dst_ref=dst.at[r + cross],
            send_sem=ctx_send.at[r, way],
            recv_sem=ctx_recv.at[r, way],
            device_id=beside((1, -1)[way], cross),
            device_id_type=MESH,
        )

    def ctx_both(r, way):
        if not fused:
            return ctx_copy(r, way, 0)
        ref = (in_s, in_g)[way]
        return pltpu.make_async_remote_copy(
            src_ref=ref,
            dst_ref=ref,
            send_sem=ctx_send.at[r, way],
            recv_sem=ctx_recv.at[r, way],
            device_id=mate,
            device_id_type=MESH,
        )

    def ctx_start(r):
        @pl.when(me < n_ctx - 1)
        def _():
            for cross in range(beside_count):
                ctx_copy(r, 0, cross).start()

        @pl.when(me > 0)
        def _():
            for cross in range(beside_count):
                ctx_copy(r, 1, cross).start()

    def ctx_wait(r):
        @pl.when(me > 0)
        def _():
            ctx_both(r, 0).wait_recv()

        @pl.when(me < n_ctx - 1)
        def _():
            ctx_both(r, 1).wait_recv()

    def ctx_done(r):
        @pl.when(me < n_ctx - 1)
        def _():
            ctx_both(r, 0).wait_send()

        @pl.when(me > 0)
        def _():
            ctx_both(r, 1).wait_send()

    def mate_copy(src, dst, send, recv):
        return pltpu.make_async_remote_copy(
            src_ref=src,
            dst_ref=dst,
            send_sem=send,
            recv_sem=recv,
            device_id=mate,
            device_id_type=MESH,
        )

    def scaled_copy():
        return mate_copy(scaled, other_scaled, scaled_sem.at[0], scaled_sem.at[1])

    def pair_copy(chunk):
        return mate_copy(
            part.at[chunk, 1 - core], pair_in.at[chunk], pair_send.at[0], pair_recv.at[chunk]
        )

    def chip_copy(chunk, d):
        to = lax.rem(chip + d, chips)
        return pltpu.make_async_remote_copy(
            src_ref=near.at[chunk, to],
            dst_ref=chip_in.at[chunk - hopping, d - 1],
            send_sem=chip_send.at[0],
            recv_sem=chip_recv.at[chunk - hopping],
            device_id={"head": to * 2 + core},
            device_id_type=MESH,
        )

    def far_copy(chunk, d):
        to = lax.rem(chip + d, chips)
        return pltpu.make_async_remote_copy(
            src_ref=far.at[to, chunk],
            dst_ref=far_in.at[d - 1, chunk],
            send_sem=far_sem.at[0],
            recv_sem=far_sem.at[1],
            device_id={"head": to * 2 + core},
            device_id_type=MESH,
        )

    def hop_copy(chunk, hop, way):
        src, dst = (hop1_out, hop1_in) if hop == 0 else (hop2_out, hop2_in)
        to = chip ^ (1 + (way + hop) % 2)
        return pltpu.make_async_remote_copy(
            src_ref=src.at[chunk, way],
            dst_ref=dst.at[chunk, way],
            send_sem=hop_send.at[hop],
            recv_sem=hop_recv.at[chunk, hop],
            device_id={"head": to * 2 + core},
            device_id_type=MESH,
        )

    def hop_both(chunk, hop):
        dst = hop1_in if hop == 0 else hop2_in
        return mate_copy(dst.at[chunk], dst.at[chunk], hop_send.at[hop], hop_recv.at[chunk, hop])

    loads[2].wait()
    loads[3].wait()
    loads[4].wait()
    loads[5].wait()
    state = jnp.zeros((width_p, width_n), F32)
    carry = jnp.zeros((width_p, width_n), F32)
    for k in range(blocks):
        s_ref[k] = state
        b_k = cut2(b_ref, k)
        hi, lo = split(cut(x_ref, k).astype(F32) * wdt8[k : k + 1])
        state = dall8[k : k + 1] * state + mm(lanes(hi, lo), lanes(b_k, b_k), 1, 1)
        j = blocks - 1 - k
        gz_ref[j] = carry
        c_j = cut2(c_ref, j)
        hi, lo = split(cut(g_ref, j).astype(F32) * din8[j : j + 1])
        carry = dall8[j : j + 1] * carry + mm(lanes(hi, lo), lanes(c_j, c_j), 1, 1)
    out_s[0] = state
    out_g[0] = carry
    meet()
    ctx_start(0)

    def put(k, way, value):
        if fused:
            chunk, lo = k // 2, (k % 2) * Q
            for h in range(n_head):
                at = (chunk, h % 2, h // 2, slice(way * each, (way + 1) * each), slice(lo, lo + Q))
                part[at] = value[h * each : (h + 1) * each]
        else:
            ref = (gb_ref, gc_ref)[way]
            ref[:, k * Q : (k + 1) * Q] = value

    def scale(k):
        to_start = cut(g_ref, k).astype(F32) * (din8[k : k + 1] * ahead[k])
        to_end = cut(x_ref, k).astype(F32) * (wdt8[k : k + 1] * behind[k])
        scaled[:, k * Q : (k + 1) * Q] = jnp.where(first8[k : k + 1], to_start, to_end)

    def local_w(k):
        x_k, g_k, b_k, c_k = cut(x_ref, k), cut(g_ref, k), cut2(b_ref, k), cut2(c_ref, k)
        mask = lower & (seg_t[:, k : k + 1] == seg8[k : k + 1])
        gap = jnp.where(mask, cum_t[:, k : k + 1] - cum8[k : k + 1], 0.0)
        ddt = jnp.where(mask, jnp.exp(gap), 0.0) * dt8[k : k + 1]
        ddt_ref[k] = ddt
        w_hi, w_lo = split(mm(g_k, x_k, 0, 0) * ddt)
        grad_b = mm(lanes(c_k, c_k), rows(w_hi, w_lo), 1, 0)
        grad_c = mm(lanes(b_k, b_k), lanes(w_hi, w_lo), 1, 1)
        if k < blocks - 1:
            z_hi, z_lo = split(gz_ref[k])
            grad_b += mm(rows(z_hi, z_lo), rows(x_k, x_k), 0, 0) * wdt8[k : k + 1]
        if k > 0:
            s_hi, s_lo = split(s_ref[k])
            grad_c += mm(rows(s_hi, s_lo), rows(g_k, g_k), 0, 0) * din8[k : k + 1]
        put(k, 0, grad_b)
        put(k, 1, grad_c)

    def far_w(k, state_in, grad_in):
        x_k, g_k = cut(x_ref, k), cut(g_ref, k)
        at = slice(k * Q, (k + 1) * Q)
        z_hi, z_lo = split(grad_in)
        s_hi, s_lo = split(state_in)
        wdt, din = wdt8[k : k + 1] * behind[k], din8[k : k + 1] * ahead[k]
        gb_ref[:, at] += mm(rows(z_hi, z_lo), rows(x_k, x_k), 0, 0) * wdt
        gc_ref[:, at] += mm(rows(s_hi, s_lo), rows(g_k, g_k), 0, 0) * din

    diffs, qs, tails = [None] * blocks, [None] * blocks, [None] * blocks

    def halve():
        hi, lo = split(rows(scaled[...], other_scaled[...]))
        halves[0] = hi
        halves[1] = lo

    def turned(ref):
        both = rows(ref[0], ref[1]).T
        low = [both[2 * h * each : (2 * h + 1) * each] for h in range(chips)]
        high = [both[(2 * h + 1) * each : (2 * h + 2) * each] for h in range(chips)]
        return jnp.where(core == 0, rows(*low), rows(*high))

    def chunk_first(chunk):
        return lanes(*[first8[k : k + 1].astype(F32) for k in (2 * chunk, 2 * chunk + 1)]) > 0

    def reach(chunk, states):
        at = slice(chunk * 2 * Q, (chunk + 1) * 2 * Q)
        hi, lo = halves[0, :, at], halves[1, :, at]
        both = mm(states, rows(hi, lo, hi), 1, 0)
        half = width_n // 2
        first = chunk_first(chunk)
        if chunk < early:
            value = jnp.where(first, both[half:], both[:half])
            for h in range(chips):
                far[h, chunk] = value[h * each : (h + 1) * each]
            for d in range(1, chips):
                far_copy(chunk, d).start()
            return
        pair_copy(chunk).wait_recv()
        sums = jnp.where(first, 0.0, both[:half]), jnp.where(first, both[half:], 0.0)
        for h in range(chips):
            for way in range(2):
                at = (h, of(way))
                local_sum = part[(chunk, core) + at] + pair_in[(chunk,) + at]
                near[(chunk,) + at] = local_sum + sums[way][h * each : (h + 1) * each]
        leave(chunk)

    def outer(k, state_in, grad_in):
        x_k, g_k, b_k, c_k = cut(x_ref, k), cut(g_ref, k), cut2(b_ref, k), cut2(c_ref, k)
        s_k = s_ref[k] + ahead[k] * state_in
        gz = gz_ref[k] + behind[k] * grad_in
        if k + 1 < blocks:
            s_end = s_ref[k + 1] + ahead[k + 1] * state_in
        else:
            s_end = out_s[0] + decay_dev * state_in
        tails[k] = jnp.sum(jnp.sum(gz * s_end, axis=0, keepdims=True), axis=1, keepdims=True)
        a_hi, a_lo = split(mm(c_k, b_k, 0, 0) * ddt_ref[k])
        s_hi, s_lo = split(s_k)
        z_hi, z_lo = split(gz)
        din, wdt = din8[k : k + 1], wdt8[k : k + 1]
        y = mm(lanes(x_k, x_k), lanes(a_hi, a_lo), 1, 1)
        y = y + mm(lanes(s_hi, s_lo), rows(c_k, c_k), 1, 0) * din
        v = mm(lanes(g_k, g_k), rows(a_hi, a_lo), 1, 0)
        v = v + mm(lanes(z_hi, z_lo), rows(b_k, b_k), 1, 0) * wdt
        x_f, g_f = x_k.astype(F32), g_k.astype(F32)
        mixed_ref[0, :, k * Q : (k + 1) * Q] = (y + skip * x_f).astype(BF16)
        gx_ref[0, :, k * Q : (k + 1) * Q] = (v + skip * g_f).astype(BF16)
        q_k = jnp.sum(x_f * v, axis=0, keepdims=True)
        qs[k] = q_k
        diffs[k] = jnp.sum(g_f * y, axis=0, keepdims=True) - q_k

    def of(way):
        return slice(way * each, (way + 1) * each)

    def second(chunk):
        pair_copy(chunk).wait_recv()
        near[chunk] = part[chunk, core] + pair_in[chunk]
        leave(chunk)

    def leave(chunk):
        if chunk < hopping:
            for way in range(2):
                hop1_out[chunk, way, 0] = near[chunk, chip ^ (1 + way), of(way)]
                hop1_out[chunk, way, 1] = near[chunk, chip ^ 3, of(way)]
                hop_copy(chunk, 0, way).start()
        else:
            for d in range(1, chips):
                chip_copy(chunk, d).start()

    def third(chunk):
        hop_both(chunk, 0).wait_recv()
        for way in range(2):
            hop2_out[chunk, way] = near[chunk, chip ^ (2 - way), of(way)] + hop1_in[chunk, way, 1]
            hop_copy(chunk, 1, way).start()

    def last(chunk):
        at = slice(chunk * 2 * Q, (chunk + 1) * 2 * Q)
        if chunk < hopping:
            hop_both(chunk, 1).wait_recv()
            sums = [
                near[chunk, chip, of(way)] + hop1_in[chunk, way, 0] + hop2_in[chunk, way]
                for way in range(2)
            ]
        else:
            whole = chip_in.at[chunk - hopping]
            mate_copy(whole, whole, chip_send.at[0], chip_recv.at[chunk - hopping]).wait_recv()
            total = near[chunk, chip]
            for d in range(1, chips):
                total = total + chip_in[chunk - hopping, d - 1]
            sums = [total[of(way)] for way in range(2)]
        if chunk < early:
            more = far[chip, chunk]
            for d in range(1, chips):
                more = more + far_in[d - 1, chunk]
            first = chunk_first(chunk)
            sums[0] += jnp.where(first, 0.0, more)
            sums[1] += jnp.where(first, more, 0.0)
        gb_ref[:, at] = sums[0]
        gc_ref[:, at] = sums[1]

    def all_sent():
        mate_copy(pair_in, pair_in, pair_send.at[0], pair_recv.at[0]).wait_send()
        scaled_copy().wait_send()
        if early:
            mate_copy(far_in, far_in, far_sem.at[0], far_sem.at[1]).wait_send()
        if hopping:
            mate_copy(hop1_out, hop1_out, hop_send.at[0], hop_recv.at[0, 0]).wait_send()
            mate_copy(hop2_out, hop2_out, hop_send.at[1], hop_recv.at[0, 0]).wait_send()
        if hopping < chunks:
            mate_copy(chip_in, chip_in, chip_send.at[0], chip_recv.at[0]).wait_send()

    if fused:
        for k in range(blocks):
            scale(k)
        scaled_copy().start()
        for k in range(blocks):
            local_w(k)
            if k % 2 == 1:
                pair_copy(k // 2).start()
        for chunk in range(early):
            second(chunk)
        scaled_copy().wait_recv()
        halve()
        ctx_wait(0)
        state_in = in_s[0]
        grad_in = in_g[0]
        hi, lo = split(rows(turned(in_g), turned(in_s)))
        states = lanes(hi, hi, lo)
        for chunk in [*range(early, chunks), *range(early)]:
            reach(chunk, states)
        for k in range(blocks):
            outer(k, state_in, grad_in)
            for chunk in range(hopping):
                if TURN[chunk] == k:
                    third(chunk)
    else:
        for k in range(blocks):
            local_w(k)
        ctx_wait(0)
        for r in range(1, hops):
            out_s[r] = out_s[0] + decay_dev * in_s[r - 1]
            out_g[r] = out_g[0] + decay_dev * in_g[r - 1]
            ctx_start(r)
            ctx_wait(r)
        state_in = in_s[hops - 1]
        grad_in = in_g[hops - 1]
        for k in range(blocks):
            far_w(k, state_in, grad_in)
            outer(k, state_in, grad_in)

    q8 = rows(*qs)
    r8 = rows(*diffs)
    tail8 = rows(*tails)
    back8 = lax.dot_general(
        r8, lower_ones, (((1,), (0,)), ((), ())), precision=HIGH, preferred_element_type=F32
    )
    gdt8 = q8 / dt8 - rate * (back8 + tail8)
    for k in range(blocks):
        gdt_ref[0:1, k * Q : (k + 1) * Q] = gdt8[k : k + 1]

    for r in range(hops):
        ctx_done(r)
    if fused:
        if early:
            mate_copy(far_in, far_in, far_sem.at[0], far_sem.at[1]).wait_recv()
        for chunk in range(chunks):
            last(chunk)
        all_sent()


def move(*refs):
    count = (len(refs) - 1) // 2
    sem = refs[-1]
    copies = [pltpu.make_async_copy(refs[i], refs[count + i], sem.at[i]) for i in range(count)]
    for copy in copies:
        copy.start()
    for copy in copies:
        copy.wait()


def per_device(n_ctx, n_head, inputs, dt, decay_rate, skip, b_proj, c_proj, lengths, grad_out):
    _, width_p, local = inputs.shape
    width_n = b_proj.shape[0]
    longest = n_ctx * local // 4
    hops = max(1, min(n_ctx - 1, (longest - 2) // local + 1))
    each = width_n // n_head
    blocks = local // Q
    chips = n_head // 2
    chunks = blocks // 2
    fused = each % 8 == 0 and longest <= local and blocks % 2 == 0
    hopping = max(0, chunks - STRAIGHT) if chips == 4 else 0
    early = min(EARLY, chunks)
    vmem = pl.BlockSpec(memory_space=pltpu.VMEM)
    smem = pl.BlockSpec(memory_space=pltpu.SMEM)
    anywhere = pl.BlockSpec(memory_space=pl.ANY)
    result = pltpu.VMEM if fused else jax.ShapeDtypeStruct
    grad_rows = each if fused else width_n
    inward = hops + 1 if fused else hops
    scratch = [
        pltpu.SMEM(lengths.shape, lengths.dtype),
        pltpu.VMEM(inputs.shape, BF16),
        pltpu.VMEM(dt.shape, F32),
        pltpu.VMEM(b_proj.shape, BF16),
        pltpu.VMEM(c_proj.shape, BF16),
        pltpu.VMEM(grad_out.shape, BF16),
        pltpu.SemaphoreType.DMA((6,)),
        pltpu.VMEM((blocks, width_p, width_n), F32),
        pltpu.VMEM((blocks, width_p, width_n), F32),
        pltpu.VMEM((blocks, Q, Q), F32),
        pltpu.VMEM((hops, width_p, width_n), F32),
        pltpu.VMEM((hops, width_p, width_n), F32),
        pltpu.VMEM((inward, width_p, width_n), F32),
        pltpu.VMEM((inward, width_p, width_n), F32),
        pltpu.SemaphoreType.DMA((hops, 2)),
        pltpu.SemaphoreType.DMA((hops, 2)),
    ]
    if fused:
        straight = max(1, chunks - hopping)
        held = max(1, hopping)
        scratch += [
            pltpu.VMEM((chunks, 2, chips, 2 * each, 2 * Q), F32),
            pltpu.VMEM((chunks, chips, 2 * each, 2 * Q), F32),
            pltpu.VMEM((chunks, chips, 2 * each, 2 * Q), F32),
            pltpu.VMEM((held, 2, 2, each, 2 * Q), F32),
            pltpu.VMEM((held, 2, 2, each, 2 * Q), F32),
            pltpu.VMEM((held, 2, each, 2 * Q), F32),
            pltpu.VMEM((held, 2, each, 2 * Q), F32),
            pltpu.VMEM((straight, chips - 1, 2 * each, 2 * Q), F32),
            pltpu.VMEM((chips, max(1, early), each, 2 * Q), F32),
            pltpu.VMEM((chips - 1, max(1, early), each, 2 * Q), F32),
            pltpu.VMEM((width_p, local), F32),
            pltpu.VMEM((width_p, local), F32),
            pltpu.VMEM((2, 2 * width_p, local), BF16),
            pltpu.SemaphoreType.DMA((1,)),
            pltpu.SemaphoreType.DMA((chunks,)),
            pltpu.SemaphoreType.DMA((2,)),
            pltpu.SemaphoreType.DMA((held, 2)),
            pltpu.SemaphoreType.DMA((1,)),
            pltpu.SemaphoreType.DMA((straight,)),
            pltpu.SemaphoreType.DMA((2,)),
            pltpu.SemaphoreType.DMA((2,)),
        ]
    mixed, gx, gdt, gb, gc = pl.pallas_call(
        functools.partial(kernel, (n_ctx, n_head, hops, fused, lengths.shape[0], hopping, early)),
        out_shape=(
            result(inputs.shape, BF16),
            result(inputs.shape, BF16),
            result(dt.shape, F32),
            result((grad_rows, local), F32),
            result((grad_rows, local), F32),
        ),
        in_specs=[smem, smem] + [anywhere] * 6,
        out_specs=(vmem,) * 5,
        scratch_shapes=scratch,
        compiler_params=pltpu.CompilerParams(collective_id=0, has_side_effects=True),
    )(decay_rate, skip, lengths, inputs, dt, b_proj, c_proj, grad_out)
    if not fused:
        gb = lax.psum_scatter(gb, "head", scatter_dimension=0, tiled=True)
        gc = lax.psum_scatter(gc, "head", scatter_dimension=0, tiled=True)
    results = (mixed, gx, gdt, gb, gc)
    if fused:
        results = tuple(pltpu.with_memory_space_constraint(r, pltpu.VMEM) for r in results)
    return pl.pallas_call(
        move,
        out_shape=tuple(jax.ShapeDtypeStruct(r.shape, r.dtype) for r in results),
        in_specs=[vmem if fused else anywhere] * 5,
        out_specs=(anywhere,) * 5,
        scratch_shapes=[pltpu.SemaphoreType.DMA((5,))],
    )(*results)


def solution(mesh):
    return jax.shard_map(
        functools.partial(per_device, mesh.shape["ctx"], mesh.shape["head"]),
        mesh=mesh,
        in_specs=(
            P("head", None, "ctx"),
            P("head", "ctx"),
            P("head"),
            P("head"),
            P(None, "ctx"),
            P(None, "ctx"),
            P(),
            P("head", None, "ctx"),
        ),
        out_specs=(
            P("head", None, "ctx"),
            P("head", None, "ctx"),
            P("head", "ctx"),
            P("head", "ctx"),
            P("head", "ctx"),
        ),
        check_vma=False,
    )
```

```python
import functools
import jax
import jax.numpy as jnp
from jax import lax
from jax.experimental import pallas as pl
from jax.experimental.pallas import tpu as pltpu
from jax.sharding import PartitionSpec as P

Q = 128
EARLY = 3
STRAIGHT = 1
SCALE_AT = 1
HIGH = lax.Precision.HIGHEST
F32 = jnp.float32
BF16 = jnp.bfloat16
MESH = pl.DeviceIdType.MESH


def mm(a, b, ca, cb):
    return lax.dot_general(a, b, (((ca,), (cb,)), ((), ())), preferred_element_type=F32)


def split(v):
    hi = v.astype(BF16)
    return hi, (v - hi.astype(F32)).astype(BF16)


def lanes(*parts):
    return jnp.concatenate(parts, axis=1)


def rows(*parts):
    return jnp.concatenate(parts, axis=0)


def kernel(cfg, rate_ref, skip_ref, len_in, x_in, dt_in, b_in, c_in, g_in, *refs):
    n_ctx, n_head, hops, fused, ndoc, hopping, early = cfg
    mixed_ref, gx_ref, gdt_ref, gb_ref, gc_ref = refs[:5]
    len_ref, x_ref, dt_ref, b_ref, c_ref, g_ref, load_sem = refs[5:12]
    (s_ref, gz_ref, ddt_ref, out_s, out_g, in_s, in_g, ctx_send, ctx_recv) = refs[12:21]
    if fused:
        part, pair_in, near, hop1_out, hop1_in, hop2_out, hop2_in, chip_in = refs[21:29]
        far, far_in, turn_out, turn_in, scaled, other_scaled, halves = refs[29:36]
        pair_send, pair_recv, hop_send, hop_recv, chip_send, chip_recv, far_send, far_recv, scaled_sem, cross_send, cross_recv = refs[36:]
    width_p = x_ref.shape[1]
    local = x_ref.shape[2]
    width_n = b_ref.shape[0]
    blocks = local // Q
    chunks = blocks // 2
    each = width_n // n_head
    me = lax.axis_index("ctx")
    head = lax.axis_index("head")
    chips = n_head // 2
    core = lax.rem(head, 2)
    chip = head // 2
    mate = {"head": chip * 2 + 1 - core}

    barrier = pltpu.get_barrier_semaphore()

    def beside(step, cross):
        to = {"ctx": me + step}
        if cross:
            to.update(mate)
        return to

    for cross in range(2 if fused else 1):

        @pl.when(me > 0)
        def _():
            pl.semaphore_signal(barrier, inc=1, device_id=beside(-1, cross), device_id_type=MESH)

        @pl.when(me < n_ctx - 1)
        def _():
            pl.semaphore_signal(barrier, inc=1, device_id=beside(1, cross), device_id_type=MESH)

    if fused:
        pl.semaphore_signal(barrier, inc=1, device_id=mate, device_id_type=MESH)
        for d in range(1, chips):
            to = lax.rem(chip + d, chips) * 2 + core
            pl.semaphore_signal(barrier, inc=1, device_id={"head": to}, device_id_type=MESH)

    pairs = (
        (dt_in, dt_ref),
        (len_in, len_ref),
        (x_in, x_ref),
        (b_in, b_ref),
        (g_in, g_ref),
        (c_in, c_ref),
    )
    loads = [
        pltpu.make_async_copy(src, dst, load_sem.at[i]) for i, (src, dst) in enumerate(pairs)
    ]
    for load in loads:
        load.start()

    rate = rate_ref[0]
    skip = skip_ref[0]
    offset = me * local

    row_i = lax.broadcasted_iota(jnp.int32, (Q, Q), 0)
    col_j = lax.broadcasted_iota(jnp.int32, (Q, Q), 1)
    lower = row_i >= col_j
    lower_ones = lower.astype(F32)
    loads[0].wait()
    dt8 = rows(*[dt_ref[0:1, k * Q : (k + 1) * Q] for k in range(blocks)])
    log8 = -rate * dt8
    log_hi, log_rest = log8.astype(BF16), log8 - log8.astype(BF16).astype(F32)
    log_parts = lanes(log_hi, *split(log_rest))
    ones3 = lanes(*[lower.astype(BF16)] * 3)
    cum8 = mm(log_parts, ones3, 1, 1)
    cum_t = mm(ones3, log_parts, 1, 1)
    end8 = cum8[:, Q - 1 : Q]

    loads[1].wait()
    ends = []
    total = len_ref[0]
    for j in range(ndoc - 1):
        ends.append(total)
        total = total + len_ref[j + 1]

    def segment_of(pos):
        seg = jnp.zeros(pos.shape, jnp.int32)
        for end in ends:
            seg = seg + (pos >= end).astype(jnp.int32)
        return seg

    pos8 = (
        offset
        + lax.broadcasted_iota(jnp.int32, (blocks, Q), 0) * Q
        + lax.broadcasted_iota(jnp.int32, (blocks, Q), 1)
    )
    pos_t = (
        offset
        + lax.broadcasted_iota(jnp.int32, (Q, blocks), 1) * Q
        + lax.broadcasted_iota(jnp.int32, (Q, blocks), 0)
    )
    seg8 = segment_of(pos8)
    seg_t = segment_of(pos_t)
    before8 = jnp.where(pos8 == 0, -1, segment_of(pos8 - 1))
    prev8 = before8[:, 0:1]
    last8 = seg8[:, Q - 1 : Q]
    first8 = seg8 == before8[0:1, 0:1]

    din8 = jnp.where(seg8 == prev8, jnp.exp(cum8), 0.0)
    wdt8 = jnp.where(seg8 == last8, jnp.exp(end8 - cum8), 0.0) * dt8
    dall8 = jnp.where(last8 == prev8, jnp.exp(end8), 0.0)

    def cut(ref, k):
        return ref[0, :, k * Q : (k + 1) * Q]

    def cut2(ref, k):
        return ref[:, k * Q : (k + 1) * Q]

    ahead = [None] * blocks
    prod = jnp.ones((1, 1), F32)
    for k in range(blocks):
        ahead[k] = prod
        prod = prod * dall8[k : k + 1]
    decay_dev = prod
    behind = [None] * blocks
    prod = jnp.ones((1, 1), F32)
    for k in reversed(range(blocks)):
        behind[k] = prod
        prod = prod * dall8[k : k + 1]

    @pl.when(me == 0)
    def _():
        in_s[...] = jnp.zeros_like(in_s)

    @pl.when(me == n_ctx - 1)
    def _():
        in_g[...] = jnp.zeros_like(in_g)

    at_end = (me == 0) | (me == n_ctx - 1)
    peers = chips if fused else 0
    beside_count = 2 if fused else 1

    def meet():
        @pl.when(at_end)
        def _():
            pl.semaphore_wait(barrier, peers + beside_count)

        @pl.when(jnp.logical_not(at_end))
        def _():
            pl.semaphore_wait(barrier, peers + 2 * beside_count)

    def mate_copy(src, dst, send, recv):
        return pltpu.make_async_remote_copy(
            src_ref=src,
            dst_ref=dst,
            send_sem=send,
            recv_sem=recv,
            device_id=mate,
            device_id_type=MESH,
        )

    def ctx_copy(r, way):
        src, dst = (out_s, in_s) if way == 0 else (out_g, in_g)
        return pltpu.make_async_remote_copy(
            src_ref=src.at[r],
            dst_ref=dst.at[r],
            send_sem=ctx_send.at[r, way],
            recv_sem=ctx_recv.at[r, way],
            device_id=beside((1, -1)[way], 0),
            device_id_type=MESH,
        )

    def cross_copy(way):
        src, dst = (out_s, in_s) if way == 0 else (out_g, in_g)
        return pltpu.make_async_remote_copy(
            src_ref=src.at[0],
            dst_ref=dst.at[1],
            send_sem=cross_send.at[way],
            recv_sem=cross_recv.at[way],
            device_id=beside((1, -1)[way], 1),
            device_id_type=MESH,
        )

    def hand_copy(way):
        ref = (in_s, in_g)[way]
        return mate_copy(ref.at[0], ref.at[1], cross_send.at[way], cross_recv.at[way])

    def each_way(leaving, act):
        here = (me < n_ctx - 1, me > 0) if leaving else (me > 0, me < n_ctx - 1)
        for way in range(2):

            @pl.when(here[way])
            def _():
                act(way)

    def ctx_start(r):
        each_way(True, lambda way: ctx_copy(r, way).start())

    def ctx_wait(r):
        each_way(False, lambda way: ctx_copy(r, way).wait_recv())

    def ctx_done(r):
        each_way(True, lambda way: ctx_copy(r, way).wait_send())

    def cross_start():
        @pl.when(core == 0)
        def _():
            each_way(True, lambda way: cross_copy(way).start())

    def hand_over():
        ctx_wait(0)

        @pl.when(core == 1)
        def _():
            each_way(False, lambda way: hand_copy(way).start())

    def cross_wait():
        each_way(False, lambda way: cross_copy(way).wait_recv())

    def cross_done():
        @pl.when(core == 0)
        def _():
            each_way(True, lambda way: cross_copy(way).wait_send())

        @pl.when(core == 1)
        def _():
            each_way(False, lambda way: hand_copy(way).wait_send())

    def scaled_copy():
        return mate_copy(scaled, other_scaled, scaled_sem.at[0], scaled_sem.at[1])

    def pair_copy(chunk):
        return mate_copy(
            part.at[chunk, 1 - core], pair_in.at[chunk], pair_send.at[0], pair_recv.at[chunk]
        )

    first_off = jnp.where(chip == 0, 1, chip)
    offs = (first_off, jnp.where(first_off == 1, 2, 1), jnp.where(first_off == 3, 2, 3))

    def chip_copy(chunk, i):
        to = chip ^ offs[i]
        return pltpu.make_async_remote_copy(
            src_ref=near.at[chunk, to],
            dst_ref=chip_in.at[chunk - hopping, offs[i] - 1],
            send_sem=chip_send.at[0],
            recv_sem=chip_recv.at[chunk - hopping],
            device_id={"head": to * 2 + core},
            device_id_type=MESH,
        )

    def far_copy(chunk, i):
        to = chip ^ offs[i]
        return pltpu.make_async_remote_copy(
            src_ref=far.at[to, chunk],
            dst_ref=far_in.at[chunk, offs[i] - 1],
            send_sem=far_send.at[0],
            recv_sem=far_recv.at[chunk],
            device_id={"head": to * 2 + core},
            device_id_type=MESH,
        )

    def turn_copy(chunk, way):
        return pltpu.make_async_remote_copy(
            src_ref=turn_out.at[chunk, way],
            dst_ref=turn_in.at[chunk, way],
            send_sem=far_send.at[0],
            recv_sem=far_recv.at[chunk],
            device_id={"head": (chip ^ (1 + way)) * 2 + core},
            device_id_type=MESH,
        )

    def far_all(ref, chunk):
        return mate_copy(ref.at[chunk], ref.at[chunk], far_send.at[0], far_recv.at[chunk])

    def hop_copy(chunk, hop, way):
        src, dst = (hop1_out, hop1_in) if hop == 0 else (hop2_out, hop2_in)
        to = chip ^ (1 + (way + hop) % 2)
        return pltpu.make_async_remote_copy(
            src_ref=src.at[chunk, way],
            dst_ref=dst.at[chunk, way],
            send_sem=hop_send.at[hop],
            recv_sem=hop_recv.at[chunk, hop],
            device_id={"head": to * 2 + core},
            device_id_type=MESH,
        )

    def hop_both(chunk, hop):
        dst = hop1_in if hop == 0 else hop2_in
        return mate_copy(dst.at[chunk], dst.at[chunk], hop_send.at[hop], hop_recv.at[chunk, hop])

    loads[2].wait()
    loads[3].wait()
    loads[4].wait()
    loads[5].wait()
    state = jnp.zeros((width_p, width_n), F32)
    carry = jnp.zeros((width_p, width_n), F32)
    for k in range(blocks):
        s_ref[k] = state
        b_k = cut2(b_ref, k)
        hi, lo = split(cut(x_ref, k).astype(F32) * wdt8[k : k + 1])
        both = mm(rows(hi, lo), b_k, 1, 1)
        state = dall8[k : k + 1] * state + (both[:width_p] + both[width_p:])
        j = blocks - 1 - k
        gz_ref[j] = carry
        c_j = cut2(c_ref, j)
        hi, lo = split(cut(g_ref, j).astype(F32) * din8[j : j + 1])
        both = mm(rows(hi, lo), c_j, 1, 1)
        carry = dall8[j : j + 1] * carry + (both[:width_p] + both[width_p:])
    out_s[0] = state
    out_g[0] = carry
    meet()
    ctx_start(0)
    if fused:
        cross_start()

    def put(k, way, value):
        if fused:
            chunk, lo = k // 2, (k % 2) * Q
            for h in range(n_head):
                for half in range(2):
                    row = half * each + way * (each // 2)
                    at = (slice(row, row + each // 2), slice(lo, lo + Q))
                    row = h * each + half * (each // 2)
                    part[(chunk, h % 2, h // 2) + at] = value[row : row + each // 2]
        else:
            ref = (gb_ref, gc_ref)[way]
            ref[:, k * Q : (k + 1) * Q] = value

    def scale(k):
        to_start = cut(g_ref, k).astype(F32) * (din8[k : k + 1] * ahead[k])
        to_end = cut(x_ref, k).astype(F32) * (wdt8[k : k + 1] * behind[k])
        scaled[:, k * Q : (k + 1) * Q] = jnp.where(first8[k : k + 1], to_start, to_end)

    def local_w(k):
        x_k, g_k, b_k, c_k = cut(x_ref, k), cut(g_ref, k), cut2(b_ref, k), cut2(c_ref, k)
        mask = lower & (seg_t[:, k : k + 1] == seg8[k : k + 1])
        gap = jnp.where(mask, cum_t[:, k : k + 1] - cum8[k : k + 1], 0.0)
        ddt = jnp.where(mask, jnp.exp(gap), 0.0) * dt8[k : k + 1]
        ddt_ref[k] = ddt
        w_hi, w_lo = split(mm(g_k, x_k, 0, 0) * ddt)
        grad_b = mm(lanes(c_k, c_k), rows(w_hi, w_lo), 1, 0)
        grad_c = mm(lanes(b_k, b_k), lanes(w_hi, w_lo), 1, 1)
        if k < blocks - 1:
            z_hi, z_lo = split(gz_ref[k])
            grad_b += mm(rows(z_hi, z_lo), rows(x_k, x_k), 0, 0) * wdt8[k : k + 1]
        if k > 0:
            s_hi, s_lo = split(s_ref[k])
            grad_c += mm(rows(s_hi, s_lo), rows(g_k, g_k), 0, 0) * din8[k : k + 1]
        put(k, 0, grad_b)
        put(k, 1, grad_c)

    def far_w(k, state_in, grad_in):
        x_k, g_k = cut(x_ref, k), cut(g_ref, k)
        at = slice(k * Q, (k + 1) * Q)
        z_hi, z_lo = split(grad_in)
        s_hi, s_lo = split(state_in)
        wdt, din = wdt8[k : k + 1] * behind[k], din8[k : k + 1] * ahead[k]
        gb_ref[:, at] += mm(rows(z_hi, z_lo), rows(x_k, x_k), 0, 0) * wdt
        gc_ref[:, at] += mm(rows(s_hi, s_lo), rows(g_k, g_k), 0, 0) * din

    diffs, qs, tails = [None] * blocks, [None] * blocks, [None] * blocks

    def halve():
        hi, lo = split(rows(scaled[...], other_scaled[...]))
        halves[0] = hi
        halves[1] = lo

    def turned(ref):
        both = rows(ref[0], ref[1]).T
        low = [both[2 * h * each : (2 * h + 1) * each] for h in range(chips)]
        high = [both[(2 * h + 1) * each : (2 * h + 2) * each] for h in range(chips)]
        return jnp.where(core == 0, rows(*low), rows(*high))

    def chunk_first(chunk):
        return lanes(*[first8[k : k + 1].astype(F32) for k in (2 * chunk, 2 * chunk + 1)]) > 0

    def reach(chunk, states):
        at = slice(chunk * 2 * Q, (chunk + 1) * 2 * Q)
        hi, lo = halves[0, :, at], halves[1, :, at]
        both = mm(states, rows(hi, lo, hi), 1, 0)
        half = width_n // 2
        first = chunk_first(chunk)
        if chunk < early:
            value = jnp.where(first, both[half:], both[:half])
            for h in range(chips):
                far[h, chunk] = value[h * each : (h + 1) * each]

            @pl.when(core == 1)
            def _():
                for way in range(2):
                    turn_out[chunk, way, 0] = far[chip ^ (1 + way), chunk, half_of(way)]
                    turn_out[chunk, way, 1] = far[chip ^ 3, chunk, half_of(way)]
                    turn_copy(chunk, way).start()

            return
        pair_copy(chunk).wait_recv()
        sums = jnp.where(first, 0.0, both[:half]), jnp.where(first, both[half:], 0.0)
        for h in range(chips):
            for way in range(2):
                row = h * each + way * (each // 2)
                more = rows(*[value[row : row + each // 2] for value in sums])
                at = (h, of(way))
                near[(chunk,) + at] = part[(chunk, core) + at] + pair_in[(chunk,) + at] + more

    def outer(k, state_in, grad_in):
        x_k, g_k, b_k, c_k = cut(x_ref, k), cut(g_ref, k), cut2(b_ref, k), cut2(c_ref, k)
        s_k = s_ref[k] + ahead[k] * state_in
        gz = gz_ref[k] + behind[k] * grad_in
        if k + 1 < blocks:
            s_end = s_ref[k + 1] + ahead[k + 1] * state_in
        else:
            s_end = out_s[0] + decay_dev * state_in
        tails[k] = jnp.sum(jnp.sum(gz * s_end, axis=0, keepdims=True), axis=1, keepdims=True)
        a_hi, a_lo = split(mm(c_k, b_k, 0, 0) * ddt_ref[k])
        s_hi, s_lo = split(s_k)
        z_hi, z_lo = split(gz)
        din, wdt = din8[k : k + 1], wdt8[k : k + 1]
        y = mm(lanes(x_k, x_k), lanes(a_hi, a_lo), 1, 1)
        y = y + mm(lanes(s_hi, s_lo), rows(c_k, c_k), 1, 0) * din
        v = mm(lanes(g_k, g_k), rows(a_hi, a_lo), 1, 0)
        v = v + mm(lanes(z_hi, z_lo), rows(b_k, b_k), 1, 0) * wdt
        x_f, g_f = x_k.astype(F32), g_k.astype(F32)
        mixed_ref[0, :, k * Q : (k + 1) * Q] = (y + skip * x_f).astype(BF16)
        gx_ref[0, :, k * Q : (k + 1) * Q] = (v + skip * g_f).astype(BF16)
        q_k = jnp.sum(x_f * v, axis=0, keepdims=True)
        qs[k] = q_k
        diffs[k] = jnp.sum(g_f * y, axis=0, keepdims=True) - q_k

    def of(way):
        return slice(way * each, (way + 1) * each)

    def half_of(way):
        return slice(way * (each // 2), (way + 1) * (each // 2))

    def second(chunk):
        pair_copy(chunk).wait_recv()
        near[chunk] = part[chunk, core] + pair_in[chunk]
        leave(chunk)

    def leave(chunk):
        for way in range(2):
            hop1_out[chunk, way, 0] = near[chunk, chip ^ (1 + way), of(way)]
            hop1_out[chunk, way, 1] = near[chunk, chip ^ 3, of(way)]
            hop_copy(chunk, 0, way).start()

    def third(chunk):
        hop_both(chunk, 0).wait_recv()
        if chunk < early:

            @pl.when(core == 1)
            def _():
                far_all(turn_in, chunk).wait_recv()

        for way in range(2):
            to = chip ^ (2 - way)
            value = near[chunk, to, of(way)] + hop1_in[chunk, way, 1]
            hop2_out[chunk, way] = value
            if chunk < early:

                @pl.when(core == 1)
                def _():
                    more = far[to, chunk, half_of(way)] + turn_in[chunk, way, 1]
                    first = chunk_first(chunk)
                    both = rows(jnp.where(first, 0.0, more), jnp.where(first, more, 0.0))
                    hop2_out[chunk, way] = value + both

            hop_copy(chunk, 1, way).start()

    def last(chunk):
        if chunk < hopping:
            hop_both(chunk, 1).wait_recv()
            sums = [
                near[chunk, chip, of(way)] + hop1_in[chunk, way, 0] + hop2_in[chunk, way]
                for way in range(2)
            ]
        else:
            whole = chip_in.at[chunk - hopping]
            mate_copy(whole, whole, chip_send.at[0], chip_recv.at[chunk - hopping]).wait_recv()
            total = near[chunk, chip]
            for d in range(1, chips):
                total = total + chip_in[chunk - hopping, d - 1]
            sums = [total[of(way)] for way in range(2)]

        def finish(more):
            at = slice(chunk * 2 * Q, (chunk + 1) * 2 * Q)
            first = chunk_first(chunk)
            for way, value in enumerate(sums):
                to_b, to_c = value[: each // 2], value[each // 2 :]
                if more is not None:
                    to_b = to_b + jnp.where(first, 0.0, more[half_of(way)])
                    to_c = to_c + jnp.where(first, more[half_of(way)], 0.0)
                gb_ref[half_of(way), at] = to_b
                gc_ref[half_of(way), at] = to_c

        if chunk >= early:
            finish(None)
            return

        @pl.when(core == 0)
        def _():
            far_all(far_in, chunk).wait_recv()
            more = far[chip, chunk]
            for d in range(1, chips):
                more = more + far_in[chunk, d - 1]
            finish(more)

        @pl.when(core == 1)
        def _():
            finish(far[chip, chunk] + rows(turn_in[chunk, 0, 0], turn_in[chunk, 1, 0]))

    def all_sent():
        mate_copy(pair_in, pair_in, pair_send.at[0], pair_recv.at[0]).wait_send()
        scaled_copy().wait_send()
        if early:
            for which, ref in enumerate((far_in, turn_in)):

                @pl.when(core == which)
                def _():
                    mate_copy(ref, ref, far_send.at[0], far_recv.at[0]).wait_send()

        if hopping:
            mate_copy(hop1_out, hop1_out, hop_send.at[0], hop_recv.at[0, 0]).wait_send()
            mate_copy(hop2_out, hop2_out, hop_send.at[1], hop_recv.at[0, 0]).wait_send()
        if hopping < chunks:
            mate_copy(chip_in, chip_in, chip_send.at[0], chip_recv.at[0]).wait_send()

    if fused:
        for k in range(blocks):
            local_w(k)
            if k % 2 == 1:
                pair_copy(k // 2).start()
            if k == SCALE_AT:
                for j in range(blocks):
                    scale(j)
                scaled_copy().start()
        for chunk in range(early):
            second(chunk)
        scaled_copy().wait_recv()
        halve()
        hand_over()
        cross_wait()
        state_in = in_s[0]
        grad_in = in_g[0]
        hi, lo = split(rows(turned(in_g), turned(in_s)))
        states = lanes(hi, hi, lo)
        def send_far(chunk, i):
            @pl.when(core == 0)
            def _():
                far_copy(chunk, i).start()

        reach(3, states)
        chip_copy(3, 0).start()
        reach(0, states)
        send_far(0, 0)
        reach(1, states)
        send_far(1, 0)
        reach(2, states)
        send_far(2, 0)
        chip_copy(3, 1).start()
        chip_copy(3, 2).start()
        send_far(0, 1)
        send_far(0, 2)
        send_far(1, 1)
        send_far(1, 2)
        send_far(2, 1)
        send_far(2, 2)
        outer(0, state_in, grad_in)
        outer(1, state_in, grad_in)
        outer(2, state_in, grad_in)
        outer(3, state_in, grad_in)
        third(0)
        outer(4, state_in, grad_in)
        third(1)
        outer(5, state_in, grad_in)
        outer(6, state_in, grad_in)
        third(2)
        outer(7, state_in, grad_in)
    else:
        for k in range(blocks):
            local_w(k)
        ctx_wait(0)
        for r in range(1, hops):
            out_s[r] = out_s[0] + decay_dev * in_s[r - 1]
            out_g[r] = out_g[0] + decay_dev * in_g[r - 1]
            ctx_start(r)
            ctx_wait(r)
        state_in = in_s[hops - 1]
        grad_in = in_g[hops - 1]
        for k in range(blocks):
            far_w(k, state_in, grad_in)
            outer(k, state_in, grad_in)

    q8 = rows(*qs)
    r8 = rows(*diffs)
    tail8 = rows(*tails)
    back8 = lax.dot_general(
        r8, lower_ones, (((1,), (0,)), ((), ())), precision=HIGH, preferred_element_type=F32
    )
    gdt8 = q8 / dt8 - rate * (back8 + tail8)
    for k in range(blocks):
        gdt_ref[0:1, k * Q : (k + 1) * Q] = gdt8[k : k + 1]

    for r in range(hops):
        ctx_done(r)
    if fused:
        cross_done()
        for chunk in range(chunks):
            last(chunk)
        all_sent()


def move(*refs):
    count = (len(refs) - 1) // 2
    sem = refs[-1]
    copies = [pltpu.make_async_copy(refs[i], refs[count + i], sem.at[i]) for i in range(count)]
    for copy in copies:
        copy.start()
    for copy in copies:
        copy.wait()


def per_device(n_ctx, n_head, inputs, dt, decay_rate, skip, b_proj, c_proj, lengths, grad_out):
    _, width_p, local = inputs.shape
    width_n = b_proj.shape[0]
    longest = n_ctx * local // 4
    hops = max(1, min(n_ctx - 1, (longest - 2) // local + 1))
    each = width_n // n_head
    blocks = local // Q
    chips = n_head // 2
    chunks = blocks // 2
    fused = each % 16 == 0 and longest <= local and chunks == 4 and chips == 4
    hopping = chunks - STRAIGHT
    early = min(EARLY, hopping)
    vmem = pl.BlockSpec(memory_space=pltpu.VMEM)
    smem = pl.BlockSpec(memory_space=pltpu.SMEM)
    anywhere = pl.BlockSpec(memory_space=pl.ANY)
    result = pltpu.VMEM if fused else jax.ShapeDtypeStruct
    grad_rows = each if fused else width_n
    inward = hops + 1 if fused else hops
    scratch = [
        pltpu.SMEM(lengths.shape, lengths.dtype),
        pltpu.VMEM(inputs.shape, BF16),
        pltpu.VMEM(dt.shape, F32),
        pltpu.VMEM(b_proj.shape, BF16),
        pltpu.VMEM(c_proj.shape, BF16),
        pltpu.VMEM(grad_out.shape, BF16),
        pltpu.SemaphoreType.DMA((6,)),
        pltpu.VMEM((blocks, width_p, width_n), F32),
        pltpu.VMEM((blocks, width_p, width_n), F32),
        pltpu.VMEM((blocks, Q, Q), F32),
        pltpu.VMEM((hops, width_p, width_n), F32),
        pltpu.VMEM((hops, width_p, width_n), F32),
        pltpu.VMEM((inward, width_p, width_n), F32),
        pltpu.VMEM((inward, width_p, width_n), F32),
        pltpu.SemaphoreType.DMA((hops, 2)),
        pltpu.SemaphoreType.DMA((hops, 2)),
    ]
    if fused:
        straight = max(1, chunks - hopping)
        held = max(1, hopping)
        scratch += [
            pltpu.VMEM((chunks, 2, chips, 2 * each, 2 * Q), F32),
            pltpu.VMEM((chunks, chips, 2 * each, 2 * Q), F32),
            pltpu.VMEM((chunks, chips, 2 * each, 2 * Q), F32),
            pltpu.VMEM((held, 2, 2, each, 2 * Q), F32),
            pltpu.VMEM((held, 2, 2, each, 2 * Q), F32),
            pltpu.VMEM((held, 2, each, 2 * Q), F32),
            pltpu.VMEM((held, 2, each, 2 * Q), F32),
            pltpu.VMEM((straight, chips - 1, 2 * each, 2 * Q), F32),
            pltpu.VMEM((chips, max(1, early), each, 2 * Q), F32),
            pltpu.VMEM((max(1, early), chips - 1, each, 2 * Q), F32),
            pltpu.VMEM((max(1, early), 2, 2, each // 2, 2 * Q), F32),
            pltpu.VMEM((max(1, early), 2, 2, each // 2, 2 * Q), F32),
            pltpu.VMEM((width_p, local), F32),
            pltpu.VMEM((width_p, local), F32),
            pltpu.VMEM((2, 2 * width_p, local), BF16),
            pltpu.SemaphoreType.DMA((1,)),
            pltpu.SemaphoreType.DMA((chunks,)),
            pltpu.SemaphoreType.DMA((2,)),
            pltpu.SemaphoreType.DMA((held, 2)),
            pltpu.SemaphoreType.DMA((1,)),
            pltpu.SemaphoreType.DMA((straight,)),
            pltpu.SemaphoreType.DMA((1,)),
            pltpu.SemaphoreType.DMA((max(1, early),)),
            pltpu.SemaphoreType.DMA((2,)),
            pltpu.SemaphoreType.DMA((2,)),
            pltpu.SemaphoreType.DMA((2,)),
        ]
    mixed, gx, gdt, gb, gc = pl.pallas_call(
        functools.partial(kernel, (n_ctx, n_head, hops, fused, lengths.shape[0], hopping, early)),
        out_shape=(
            result(inputs.shape, BF16),
            result(inputs.shape, BF16),
            result(dt.shape, F32),
            result((grad_rows, local), F32),
            result((grad_rows, local), F32),
        ),
        in_specs=[smem, smem] + [anywhere] * 6,
        out_specs=(vmem,) * 5,
        scratch_shapes=scratch,
        compiler_params=pltpu.CompilerParams(collective_id=0, has_side_effects=True),
    )(decay_rate, skip, lengths, inputs, dt, b_proj, c_proj, grad_out)
    if not fused:
        gb = lax.psum_scatter(gb, "head", scatter_dimension=0, tiled=True)
        gc = lax.psum_scatter(gc, "head", scatter_dimension=0, tiled=True)
    results = (mixed, gx, gdt, gb, gc)
    if fused:
        results = tuple(pltpu.with_memory_space_constraint(r, pltpu.VMEM) for r in results)
    return pl.pallas_call(
        move,
        out_shape=tuple(jax.ShapeDtypeStruct(r.shape, r.dtype) for r in results),
        in_specs=[vmem if fused else anywhere] * 5,
        out_specs=(anywhere,) * 5,
        scratch_shapes=[pltpu.SemaphoreType.DMA((5,))],
    )(*results)


def solution(mesh):
    return jax.shard_map(
        functools.partial(per_device, mesh.shape["ctx"], mesh.shape["head"]),
        mesh=mesh,
        in_specs=(
            P("head", None, "ctx"),
            P("head", "ctx"),
            P("head"),
            P("head"),
            P(None, "ctx"),
            P(None, "ctx"),
            P(),
            P("head", None, "ctx"),
        ),
        out_specs=(
            P("head", None, "ctx"),
            P("head", None, "ctx"),
            P("head", "ctx"),
            P("head", "ctx"),
            P("head", "ctx"),
        ),
        check_vma=False,
    )
```

```python
import functools
import jax
import jax.numpy as jnp
from jax import lax
from jax.experimental import pallas as pl
from jax.experimental.pallas import tpu as pltpu
from jax.sharding import PartitionSpec as P

Q = 128
EARLY = 3
STRAIGHT = 0
SCALE_AT = 1
HIGH = lax.Precision.HIGHEST
F32 = jnp.float32
BF16 = jnp.bfloat16
MESH = pl.DeviceIdType.MESH


def mm(a, b, ca, cb):
    return lax.dot_general(a, b, (((ca,), (cb,)), ((), ())), preferred_element_type=F32)


def split(v):
    hi = v.astype(BF16)
    return hi, (v - hi.astype(F32)).astype(BF16)


def lanes(*parts):
    return jnp.concatenate(parts, axis=1)


def rows(*parts):
    return jnp.concatenate(parts, axis=0)


def kernel(cfg, rate_ref, skip_ref, len_in, x_in, dt_in, b_in, c_in, g_in, *refs):
    n_ctx, n_head, hops, fused, ndoc, hopping, early = cfg
    mixed_ref, gx_ref, gdt_ref, gb_ref, gc_ref = refs[:5]
    len_ref, x_ref, dt_ref, b_ref, c_ref, g_ref, load_sem = refs[5:12]
    (s_ref, gz_ref, ddt_ref, out_s, out_g, in_s, in_g, ctx_send, ctx_recv) = refs[12:21]
    if fused:
        part, pair_in, near, hop1_out, hop1_in, hop2_out, hop2_in, chip_in = refs[21:29]
        far, far_in, turn_out, turn_in, scaled, other_scaled, halves = refs[29:36]
        pair_send, pair_recv, hop_send, hop_recv, chip_send, chip_recv, far_send, far_recv, scaled_sem, cross_send, cross_recv = refs[36:]
    width_p = x_ref.shape[1]
    local = x_ref.shape[2]
    width_n = b_ref.shape[0]
    blocks = local // Q
    chunks = blocks // 2
    each = width_n // n_head
    me = lax.axis_index("ctx")
    head = lax.axis_index("head")
    chips = n_head // 2
    core = lax.rem(head, 2)
    chip = head // 2
    mate = {"head": chip * 2 + 1 - core}

    barrier = pltpu.get_barrier_semaphore()

    def beside(step, cross):
        to = {"ctx": me + step}
        if cross:
            to.update(mate)
        return to

    for cross in range(2 if fused else 1):

        @pl.when(me > 0)
        def _():
            pl.semaphore_signal(barrier, inc=1, device_id=beside(-1, cross), device_id_type=MESH)

        @pl.when(me < n_ctx - 1)
        def _():
            pl.semaphore_signal(barrier, inc=1, device_id=beside(1, cross), device_id_type=MESH)

    if fused:
        pl.semaphore_signal(barrier, inc=1, device_id=mate, device_id_type=MESH)
        for d in range(1, chips):
            to = lax.rem(chip + d, chips) * 2 + core
            pl.semaphore_signal(barrier, inc=1, device_id={"head": to}, device_id_type=MESH)

    pairs = (
        (dt_in, dt_ref),
        (len_in, len_ref),
        (x_in, x_ref),
        (b_in, b_ref),
        (g_in, g_ref),
        (c_in, c_ref),
    )
    loads = [
        pltpu.make_async_copy(src, dst, load_sem.at[i]) for i, (src, dst) in enumerate(pairs)
    ]
    for load in loads:
        load.start()

    rate = rate_ref[0]
    skip = skip_ref[0]
    offset = me * local

    row_i = lax.broadcasted_iota(jnp.int32, (Q, Q), 0)
    col_j = lax.broadcasted_iota(jnp.int32, (Q, Q), 1)
    lower = row_i >= col_j
    lower_ones = lower.astype(F32)
    loads[0].wait()
    dt8 = rows(*[dt_ref[0:1, k * Q : (k + 1) * Q] for k in range(blocks)])
    log8 = -rate * dt8
    log_hi, log_rest = log8.astype(BF16), log8 - log8.astype(BF16).astype(F32)
    log_parts = lanes(log_hi, *split(log_rest))
    ones3 = lanes(*[lower.astype(BF16)] * 3)
    cum8 = mm(log_parts, ones3, 1, 1)
    cum_t = mm(ones3, log_parts, 1, 1)
    end8 = cum8[:, Q - 1 : Q]

    loads[1].wait()
    ends = []
    total = len_ref[0]
    for j in range(ndoc - 1):
        ends.append(total)
        total = total + len_ref[j + 1]

    def segment_of(pos):
        seg = jnp.zeros(pos.shape, jnp.int32)
        for end in ends:
            seg = seg + (pos >= end).astype(jnp.int32)
        return seg

    pos8 = (
        offset
        + lax.broadcasted_iota(jnp.int32, (blocks, Q), 0) * Q
        + lax.broadcasted_iota(jnp.int32, (blocks, Q), 1)
    )
    pos_t = (
        offset
        + lax.broadcasted_iota(jnp.int32, (Q, blocks), 1) * Q
        + lax.broadcasted_iota(jnp.int32, (Q, blocks), 0)
    )
    seg8 = segment_of(pos8)
    seg_t = segment_of(pos_t)
    before8 = jnp.where(pos8 == 0, -1, segment_of(pos8 - 1))
    prev8 = before8[:, 0:1]
    last8 = seg8[:, Q - 1 : Q]
    first8 = seg8 == before8[0:1, 0:1]

    din8 = jnp.where(seg8 == prev8, jnp.exp(cum8), 0.0)
    wdt8 = jnp.where(seg8 == last8, jnp.exp(end8 - cum8), 0.0) * dt8
    dall8 = jnp.where(last8 == prev8, jnp.exp(end8), 0.0)

    def cut(ref, k):
        return ref[0, :, k * Q : (k + 1) * Q]

    def cut2(ref, k):
        return ref[:, k * Q : (k + 1) * Q]

    ahead = [None] * blocks
    prod = jnp.ones((1, 1), F32)
    for k in range(blocks):
        ahead[k] = prod
        prod = prod * dall8[k : k + 1]
    decay_dev = prod
    behind = [None] * blocks
    prod = jnp.ones((1, 1), F32)
    for k in reversed(range(blocks)):
        behind[k] = prod
        prod = prod * dall8[k : k + 1]

    @pl.when(me == 0)
    def _():
        in_s[...] = jnp.zeros_like(in_s)

    @pl.when(me == n_ctx - 1)
    def _():
        in_g[...] = jnp.zeros_like(in_g)

    at_end = (me == 0) | (me == n_ctx - 1)
    peers = chips if fused else 0
    beside_count = 2 if fused else 1

    def meet():
        @pl.when(at_end)
        def _():
            pl.semaphore_wait(barrier, peers + beside_count)

        @pl.when(jnp.logical_not(at_end))
        def _():
            pl.semaphore_wait(barrier, peers + 2 * beside_count)

    def mate_copy(src, dst, send, recv):
        return pltpu.make_async_remote_copy(
            src_ref=src,
            dst_ref=dst,
            send_sem=send,
            recv_sem=recv,
            device_id=mate,
            device_id_type=MESH,
        )

    def ctx_copy(r, way):
        src, dst = (out_s, in_s) if way == 0 else (out_g, in_g)
        return pltpu.make_async_remote_copy(
            src_ref=src.at[r],
            dst_ref=dst.at[r],
            send_sem=ctx_send.at[r, way],
            recv_sem=ctx_recv.at[r, way],
            device_id=beside((1, -1)[way], 0),
            device_id_type=MESH,
        )

    def cross_copy(way):
        src, dst = (out_s, in_s) if way == 0 else (out_g, in_g)
        return pltpu.make_async_remote_copy(
            src_ref=src.at[0],
            dst_ref=dst.at[1],
            send_sem=cross_send.at[way],
            recv_sem=cross_recv.at[way],
            device_id=beside((1, -1)[way], 1),
            device_id_type=MESH,
        )

    def hand_copy(way):
        ref = (in_s, in_g)[way]
        return mate_copy(ref.at[0], ref.at[1], cross_send.at[way], cross_recv.at[way])

    def each_way(leaving, act):
        here = (me < n_ctx - 1, me > 0) if leaving else (me > 0, me < n_ctx - 1)
        for way in range(2):

            @pl.when(here[way])
            def _():
                act(way)

    def ctx_start(r):
        each_way(True, lambda way: ctx_copy(r, way).start())

    def ctx_wait(r):
        each_way(False, lambda way: ctx_copy(r, way).wait_recv())

    def ctx_done(r):
        each_way(True, lambda way: ctx_copy(r, way).wait_send())

    def cross_start():
        @pl.when(core == 0)
        def _():
            each_way(True, lambda way: cross_copy(way).start())

    def hand_over():
        ctx_wait(0)

        @pl.when(core == 1)
        def _():
            each_way(False, lambda way: hand_copy(way).start())

    def cross_wait():
        each_way(False, lambda way: cross_copy(way).wait_recv())

    def cross_done():
        @pl.when(core == 0)
        def _():
            each_way(True, lambda way: cross_copy(way).wait_send())

        @pl.when(core == 1)
        def _():
            each_way(False, lambda way: hand_copy(way).wait_send())

    def scaled_copy():
        return mate_copy(scaled, other_scaled, scaled_sem.at[0], scaled_sem.at[1])

    def pair_copy(chunk):
        return mate_copy(
            part.at[chunk, 1 - core], pair_in.at[chunk], pair_send.at[0], pair_recv.at[chunk]
        )

    first_off = jnp.where(chip == 0, 1, chip)
    offs = (first_off, jnp.where(first_off == 1, 2, 1), jnp.where(first_off == 3, 2, 3))

    def chip_copy(chunk, i):
        to = chip ^ offs[i]
        return pltpu.make_async_remote_copy(
            src_ref=near.at[chunk, to],
            dst_ref=chip_in.at[0, offs[i] - 1],
            send_sem=chip_send.at[0],
            recv_sem=chip_recv.at[0],
            device_id={"head": to * 2 + core},
            device_id_type=MESH,
        )

    def far_copy(chunk, i):
        to = chip ^ offs[i]
        return pltpu.make_async_remote_copy(
            src_ref=far.at[to, chunk],
            dst_ref=far_in.at[chunk, offs[i] - 1],
            send_sem=far_send.at[0],
            recv_sem=far_recv.at[chunk],
            device_id={"head": to * 2 + core},
            device_id_type=MESH,
        )

    def turn_copy(chunk, way):
        return pltpu.make_async_remote_copy(
            src_ref=turn_out.at[chunk, way],
            dst_ref=turn_in.at[chunk, way],
            send_sem=far_send.at[0],
            recv_sem=far_recv.at[chunk],
            device_id={"head": (chip ^ (1 + way)) * 2 + core},
            device_id_type=MESH,
        )

    def far_all(ref, chunk):
        return mate_copy(ref.at[chunk], ref.at[chunk], far_send.at[0], far_recv.at[chunk])

    def hop_copy(chunk, hop, way):
        src, dst = (hop1_out, hop1_in) if hop == 0 else (hop2_out, hop2_in)
        to = chip ^ (1 + (way + hop) % 2)
        return pltpu.make_async_remote_copy(
            src_ref=src.at[chunk, way],
            dst_ref=dst.at[chunk, way],
            send_sem=hop_send.at[hop],
            recv_sem=hop_recv.at[chunk, hop],
            device_id={"head": to * 2 + core},
            device_id_type=MESH,
        )

    def hop_both(chunk, hop):
        dst = hop1_in if hop == 0 else hop2_in
        return mate_copy(dst.at[chunk], dst.at[chunk], hop_send.at[hop], hop_recv.at[chunk, hop])

    loads[2].wait()
    loads[3].wait()
    loads[4].wait()
    loads[5].wait()
    state = jnp.zeros((width_p, width_n), F32)
    carry = jnp.zeros((width_p, width_n), F32)
    for k in range(blocks):
        s_ref[k] = state
        b_k = cut2(b_ref, k)
        hi, lo = split(cut(x_ref, k).astype(F32) * wdt8[k : k + 1])
        both = mm(rows(hi, lo), b_k, 1, 1)
        state = dall8[k : k + 1] * state + (both[:width_p] + both[width_p:])
        j = blocks - 1 - k
        gz_ref[j] = carry
        c_j = cut2(c_ref, j)
        hi, lo = split(cut(g_ref, j).astype(F32) * din8[j : j + 1])
        both = mm(rows(hi, lo), c_j, 1, 1)
        carry = dall8[j : j + 1] * carry + (both[:width_p] + both[width_p:])
    out_s[0] = state
    out_g[0] = carry
    meet()
    ctx_start(0)
    if fused:
        cross_start()

    def put(k, way, value):
        if fused:
            chunk, lo = k // 2, (k % 2) * Q
            for h in range(n_head):
                for half in range(2):
                    row = half * each + way * (each // 2)
                    at = (slice(row, row + each // 2), slice(lo, lo + Q))
                    row = h * each + half * (each // 2)
                    part[(chunk, h % 2, h // 2) + at] = value[row : row + each // 2]
        else:
            ref = (gb_ref, gc_ref)[way]
            ref[:, k * Q : (k + 1) * Q] = value

    def scale(k):
        to_start = cut(g_ref, k).astype(F32) * (din8[k : k + 1] * ahead[k])
        to_end = cut(x_ref, k).astype(F32) * (wdt8[k : k + 1] * behind[k])
        scaled[:, k * Q : (k + 1) * Q] = jnp.where(first8[k : k + 1], to_start, to_end)

    def local_w(k):
        x_k, g_k, b_k, c_k = cut(x_ref, k), cut(g_ref, k), cut2(b_ref, k), cut2(c_ref, k)
        mask = lower & (seg_t[:, k : k + 1] == seg8[k : k + 1])
        gap = jnp.where(mask, cum_t[:, k : k + 1] - cum8[k : k + 1], 0.0)
        ddt = jnp.where(mask, jnp.exp(gap), 0.0) * dt8[k : k + 1]
        ddt_ref[k] = ddt
        w_hi, w_lo = split(mm(g_k, x_k, 0, 0) * ddt)
        grad_b = mm(lanes(c_k, c_k), rows(w_hi, w_lo), 1, 0)
        grad_c = mm(lanes(b_k, b_k), lanes(w_hi, w_lo), 1, 1)
        if k < blocks - 1:
            z_hi, z_lo = split(gz_ref[k])
            grad_b += mm(rows(z_hi, z_lo), rows(x_k, x_k), 0, 0) * wdt8[k : k + 1]
        if k > 0:
            s_hi, s_lo = split(s_ref[k])
            grad_c += mm(rows(s_hi, s_lo), rows(g_k, g_k), 0, 0) * din8[k : k + 1]
        put(k, 0, grad_b)
        put(k, 1, grad_c)

    def far_w(k, state_in, grad_in):
        x_k, g_k = cut(x_ref, k), cut(g_ref, k)
        at = slice(k * Q, (k + 1) * Q)
        z_hi, z_lo = split(grad_in)
        s_hi, s_lo = split(state_in)
        wdt, din = wdt8[k : k + 1] * behind[k], din8[k : k + 1] * ahead[k]
        gb_ref[:, at] += mm(rows(z_hi, z_lo), rows(x_k, x_k), 0, 0) * wdt
        gc_ref[:, at] += mm(rows(s_hi, s_lo), rows(g_k, g_k), 0, 0) * din

    diffs, qs, tails = [None] * blocks, [None] * blocks, [None] * blocks

    def halve():
        hi, lo = split(rows(scaled[...], other_scaled[...]))
        halves[0] = hi
        halves[1] = lo

    def turned(ref):
        both = rows(ref[0], ref[1]).T
        low = [both[2 * h * each : (2 * h + 1) * each] for h in range(chips)]
        high = [both[(2 * h + 1) * each : (2 * h + 2) * each] for h in range(chips)]
        return jnp.where(core == 0, rows(*low), rows(*high))

    def chunk_first(chunk):
        return lanes(*[first8[k : k + 1].astype(F32) for k in (2 * chunk, 2 * chunk + 1)]) > 0

    def reach(chunk, states):
        at = slice(chunk * 2 * Q, (chunk + 1) * 2 * Q)
        hi, lo = halves[0, :, at], halves[1, :, at]
        both = mm(states, rows(hi, lo, hi), 1, 0)
        half = width_n // 2
        first = chunk_first(chunk)
        if chunk < early:
            value = jnp.where(first, both[half:], both[:half])
            for h in range(chips):
                far[h, chunk] = value[h * each : (h + 1) * each]

            @pl.when(core == 1)
            def _():
                for way in range(2):
                    turn_out[chunk, way, 0] = far[chip ^ (1 + way), chunk, half_of(way)]
                    turn_out[chunk, way, 1] = far[chip ^ 3, chunk, half_of(way)]
                    turn_copy(chunk, way).start()

            return
        pair_copy(chunk).wait_recv()
        sums = jnp.where(first, 0.0, both[:half]), jnp.where(first, both[half:], 0.0)
        for h in range(chips):
            for way in range(2):
                row = h * each + way * (each // 2)
                more = rows(*[value[row : row + each // 2] for value in sums])
                at = (h, of(way))
                near[(chunk,) + at] = part[(chunk, core) + at] + pair_in[(chunk,) + at] + more

    def outer(k, state_in, grad_in):
        x_k, g_k, b_k, c_k = cut(x_ref, k), cut(g_ref, k), cut2(b_ref, k), cut2(c_ref, k)
        s_k = s_ref[k] + ahead[k] * state_in
        gz = gz_ref[k] + behind[k] * grad_in
        if k + 1 < blocks:
            s_end = s_ref[k + 1] + ahead[k + 1] * state_in
        else:
            s_end = out_s[0] + decay_dev * state_in
        tails[k] = jnp.sum(jnp.sum(gz * s_end, axis=0, keepdims=True), axis=1, keepdims=True)
        a_hi, a_lo = split(mm(c_k, b_k, 0, 0) * ddt_ref[k])
        s_hi, s_lo = split(s_k)
        z_hi, z_lo = split(gz)
        din, wdt = din8[k : k + 1], wdt8[k : k + 1]
        y = mm(lanes(x_k, x_k), lanes(a_hi, a_lo), 1, 1)
        y = y + mm(lanes(s_hi, s_lo), rows(c_k, c_k), 1, 0) * din
        v = mm(lanes(g_k, g_k), rows(a_hi, a_lo), 1, 0)
        v = v + mm(lanes(z_hi, z_lo), rows(b_k, b_k), 1, 0) * wdt
        x_f, g_f = x_k.astype(F32), g_k.astype(F32)
        mixed_ref[0, :, k * Q : (k + 1) * Q] = (y + skip * x_f).astype(BF16)
        gx_ref[0, :, k * Q : (k + 1) * Q] = (v + skip * g_f).astype(BF16)
        q_k = jnp.sum(x_f * v, axis=0, keepdims=True)
        qs[k] = q_k
        diffs[k] = jnp.sum(g_f * y, axis=0, keepdims=True) - q_k

    def of(way):
        return slice(way * each, (way + 1) * each)

    def half_of(way):
        return slice(way * (each // 2), (way + 1) * (each // 2))

    def second(chunk):
        pair_copy(chunk).wait_recv()
        near[chunk] = part[chunk, core] + pair_in[chunk]
        leave(chunk)

    def leave(chunk):
        for way in range(2):
            hop1_out[chunk, way, 0] = near[chunk, chip ^ (1 + way), of(way)]
            hop1_out[chunk, way, 1] = near[chunk, chip ^ 3, of(way)]
            hop_copy(chunk, 0, way).start()

    def third(chunk):
        hop_both(chunk, 0).wait_recv()
        if chunk < early:

            @pl.when(core == 1)
            def _():
                far_all(turn_in, chunk).wait_recv()

        for way in range(2):
            to = chip ^ (2 - way)
            value = near[chunk, to, of(way)] + hop1_in[chunk, way, 1]
            hop2_out[chunk, way] = value
            if chunk < early:

                @pl.when(core == 1)
                def _():
                    more = far[to, chunk, half_of(way)] + turn_in[chunk, way, 1]
                    first = chunk_first(chunk)
                    both = rows(jnp.where(first, 0.0, more), jnp.where(first, more, 0.0))
                    hop2_out[chunk, way] = value + both

            hop_copy(chunk, 1, way).start()

    def last(chunk):
        if chunk < early:
            last_of(chunk, False)
            return

        @pl.when(core == 0)
        def _():
            last_of(chunk, True)

        @pl.when(core == 1)
        def _():
            last_of(chunk, False)

    def last_of(chunk, straight):
        if straight:
            whole = chip_in.at[0]
            mate_copy(whole, whole, chip_send.at[0], chip_recv.at[0]).wait_recv()
            total = near[chunk, chip]
            for d in range(1, chips):
                total = total + chip_in[0, d - 1]
            sums = [total[of(way)] for way in range(2)]
        else:
            hop_both(chunk, 1).wait_recv()
            sums = [
                near[chunk, chip, of(way)] + hop1_in[chunk, way, 0] + hop2_in[chunk, way]
                for way in range(2)
            ]

        def finish(more):
            at = slice(chunk * 2 * Q, (chunk + 1) * 2 * Q)
            first = chunk_first(chunk)
            for way, value in enumerate(sums):
                to_b, to_c = value[: each // 2], value[each // 2 :]
                if more is not None:
                    to_b = to_b + jnp.where(first, 0.0, more[half_of(way)])
                    to_c = to_c + jnp.where(first, more[half_of(way)], 0.0)
                gb_ref[half_of(way), at] = to_b
                gc_ref[half_of(way), at] = to_c

        if chunk >= early:
            finish(None)
            return

        @pl.when(core == 0)
        def _():
            far_all(far_in, chunk).wait_recv()
            more = far[chip, chunk]
            for d in range(1, chips):
                more = more + far_in[chunk, d - 1]
            finish(more)

        @pl.when(core == 1)
        def _():
            finish(far[chip, chunk] + rows(turn_in[chunk, 0, 0], turn_in[chunk, 1, 0]))

    def all_sent():
        mate_copy(pair_in, pair_in, pair_send.at[0], pair_recv.at[0]).wait_send()
        scaled_copy().wait_send()
        if early:
            for which, ref in enumerate((far_in, turn_in)):

                @pl.when(core == which)
                def _():
                    mate_copy(ref, ref, far_send.at[0], far_recv.at[0]).wait_send()

        for which, count in enumerate((early, chunks)):

            @pl.when(core == which)
            def _():
                for hop, ref in enumerate((hop1_out, hop2_out)):
                    sent = ref.at[0:count]
                    mate_copy(sent, sent, hop_send.at[hop], hop_recv.at[0, 0]).wait_send()

        @pl.when(core == 0)
        def _():
            mate_copy(chip_in, chip_in, chip_send.at[0], chip_recv.at[0]).wait_send()

    if fused:
        for k in range(blocks):
            local_w(k)
            if k % 2 == 1:
                pair_copy(k // 2).start()
            if k == SCALE_AT:
                for j in range(blocks):
                    scale(j)
                scaled_copy().start()
        for chunk in range(early):
            second(chunk)
        scaled_copy().wait_recv()
        halve()
        hand_over()
        cross_wait()
        state_in = in_s[0]
        grad_in = in_g[0]
        hi, lo = split(rows(turned(in_g), turned(in_s)))
        states = lanes(hi, hi, lo)
        def send_late(i):
            @pl.when(core == 0)
            def _():
                chip_copy(chunks - 1, i).start()

            if i == 0:

                @pl.when(core == 1)
                def _():
                    leave(chunks - 1)

        def send_far(chunk, i):
            @pl.when(core == 0)
            def _():
                far_copy(chunk, i).start()

        reach(3, states)
        send_late(0)
        reach(0, states)
        send_far(0, 0)
        reach(1, states)
        send_far(1, 0)
        reach(2, states)
        send_far(2, 0)
        send_late(1)
        send_late(2)
        send_far(0, 1)
        send_far(0, 2)
        send_far(1, 1)
        send_far(1, 2)
        send_far(2, 1)
        send_far(2, 2)
        outer(0, state_in, grad_in)
        outer(1, state_in, grad_in)

        @pl.when(core == 1)
        def _():
            third(chunks - 1)

        third(0)
        outer(2, state_in, grad_in)
        outer(3, state_in, grad_in)
        third(1)
        outer(4, state_in, grad_in)
        outer(5, state_in, grad_in)
        third(2)
        outer(6, state_in, grad_in)
        outer(7, state_in, grad_in)
    else:
        for k in range(blocks):
            local_w(k)
        ctx_wait(0)
        for r in range(1, hops):
            out_s[r] = out_s[0] + decay_dev * in_s[r - 1]
            out_g[r] = out_g[0] + decay_dev * in_g[r - 1]
            ctx_start(r)
            ctx_wait(r)
        state_in = in_s[hops - 1]
        grad_in = in_g[hops - 1]
        for k in range(blocks):
            far_w(k, state_in, grad_in)
            outer(k, state_in, grad_in)

    q8 = rows(*qs)
    r8 = rows(*diffs)
    tail8 = rows(*tails)
    back8 = lax.dot_general(
        r8, lower_ones, (((1,), (0,)), ((), ())), precision=HIGH, preferred_element_type=F32
    )
    gdt8 = q8 / dt8 - rate * (back8 + tail8)
    for k in range(blocks):
        gdt_ref[0:1, k * Q : (k + 1) * Q] = gdt8[k : k + 1]

    for r in range(hops):
        ctx_done(r)
    if fused:
        cross_done()
        for chunk in range(chunks):
            last(chunk)
        all_sent()


def move(*refs):
    count = (len(refs) - 1) // 2
    sem = refs[-1]
    copies = [pltpu.make_async_copy(refs[i], refs[count + i], sem.at[i]) for i in range(count)]
    for copy in copies:
        copy.start()
    for copy in copies:
        copy.wait()


def per_device(n_ctx, n_head, inputs, dt, decay_rate, skip, b_proj, c_proj, lengths, grad_out):
    _, width_p, local = inputs.shape
    width_n = b_proj.shape[0]
    longest = n_ctx * local // 4
    hops = max(1, min(n_ctx - 1, (longest - 2) // local + 1))
    each = width_n // n_head
    blocks = local // Q
    chips = n_head // 2
    chunks = blocks // 2
    fused = each % 16 == 0 and EARLY == 3 and longest <= local and chunks == 4 and chips == 4
    hopping = chunks - STRAIGHT
    early = min(EARLY, hopping)
    vmem = pl.BlockSpec(memory_space=pltpu.VMEM)
    smem = pl.BlockSpec(memory_space=pltpu.SMEM)
    anywhere = pl.BlockSpec(memory_space=pl.ANY)
    result = pltpu.VMEM if fused else jax.ShapeDtypeStruct
    grad_rows = each if fused else width_n
    inward = hops + 1 if fused else hops
    scratch = [
        pltpu.SMEM(lengths.shape, lengths.dtype),
        pltpu.VMEM(inputs.shape, BF16),
        pltpu.VMEM(dt.shape, F32),
        pltpu.VMEM(b_proj.shape, BF16),
        pltpu.VMEM(c_proj.shape, BF16),
        pltpu.VMEM(grad_out.shape, BF16),
        pltpu.SemaphoreType.DMA((6,)),
        pltpu.VMEM((blocks, width_p, width_n), F32),
        pltpu.VMEM((blocks, width_p, width_n), F32),
        pltpu.VMEM((blocks, Q, Q), F32),
        pltpu.VMEM((hops, width_p, width_n), F32),
        pltpu.VMEM((hops, width_p, width_n), F32),
        pltpu.VMEM((inward, width_p, width_n), F32),
        pltpu.VMEM((inward, width_p, width_n), F32),
        pltpu.SemaphoreType.DMA((hops, 2)),
        pltpu.SemaphoreType.DMA((hops, 2)),
    ]
    if fused:
        straight = max(1, chunks - hopping)
        held = max(1, hopping)
        scratch += [
            pltpu.VMEM((chunks, 2, chips, 2 * each, 2 * Q), F32),
            pltpu.VMEM((chunks, chips, 2 * each, 2 * Q), F32),
            pltpu.VMEM((chunks, chips, 2 * each, 2 * Q), F32),
            pltpu.VMEM((held, 2, 2, each, 2 * Q), F32),
            pltpu.VMEM((held, 2, 2, each, 2 * Q), F32),
            pltpu.VMEM((held, 2, each, 2 * Q), F32),
            pltpu.VMEM((held, 2, each, 2 * Q), F32),
            pltpu.VMEM((straight, chips - 1, 2 * each, 2 * Q), F32),
            pltpu.VMEM((chips, max(1, early), each, 2 * Q), F32),
            pltpu.VMEM((max(1, early), chips - 1, each, 2 * Q), F32),
            pltpu.VMEM((max(1, early), 2, 2, each // 2, 2 * Q), F32),
            pltpu.VMEM((max(1, early), 2, 2, each // 2, 2 * Q), F32),
            pltpu.VMEM((width_p, local), F32),
            pltpu.VMEM((width_p, local), F32),
            pltpu.VMEM((2, 2 * width_p, local), BF16),
            pltpu.SemaphoreType.DMA((1,)),
            pltpu.SemaphoreType.DMA((chunks,)),
            pltpu.SemaphoreType.DMA((2,)),
            pltpu.SemaphoreType.DMA((held, 2)),
            pltpu.SemaphoreType.DMA((1,)),
            pltpu.SemaphoreType.DMA((straight,)),
            pltpu.SemaphoreType.DMA((1,)),
            pltpu.SemaphoreType.DMA((max(1, early),)),
            pltpu.SemaphoreType.DMA((2,)),
            pltpu.SemaphoreType.DMA((2,)),
            pltpu.SemaphoreType.DMA((2,)),
        ]
    mixed, gx, gdt, gb, gc = pl.pallas_call(
        functools.partial(kernel, (n_ctx, n_head, hops, fused, lengths.shape[0], hopping, early)),
        out_shape=(
            result(inputs.shape, BF16),
            result(inputs.shape, BF16),
            result(dt.shape, F32),
            result((grad_rows, local), F32),
            result((grad_rows, local), F32),
        ),
        in_specs=[smem, smem] + [anywhere] * 6,
        out_specs=(vmem,) * 5,
        scratch_shapes=scratch,
        compiler_params=pltpu.CompilerParams(collective_id=0, has_side_effects=True),
    )(decay_rate, skip, lengths, inputs, dt, b_proj, c_proj, grad_out)
    if not fused:
        gb = lax.psum_scatter(gb, "head", scatter_dimension=0, tiled=True)
        gc = lax.psum_scatter(gc, "head", scatter_dimension=0, tiled=True)
    results = (mixed, gx, gdt, gb, gc)
    if fused:
        results = tuple(pltpu.with_memory_space_constraint(r, pltpu.VMEM) for r in results)
    return pl.pallas_call(
        move,
        out_shape=tuple(jax.ShapeDtypeStruct(r.shape, r.dtype) for r in results),
        in_specs=[vmem if fused else anywhere] * 5,
        out_specs=(anywhere,) * 5,
        scratch_shapes=[pltpu.SemaphoreType.DMA((5,))],
    )(*results)


def solution(mesh):
    return jax.shard_map(
        functools.partial(per_device, mesh.shape["ctx"], mesh.shape["head"]),
        mesh=mesh,
        in_specs=(
            P("head", None, "ctx"),
            P("head", "ctx"),
            P("head"),
            P("head"),
            P(None, "ctx"),
            P(None, "ctx"),
            P(),
            P("head", None, "ctx"),
        ),
        out_specs=(
            P("head", None, "ctx"),
            P("head", None, "ctx"),
            P("head", "ctx"),
            P("head", "ctx"),
            P("head", "ctx"),
        ),
        check_vma=False,
    )
```

```python
import functools
import jax
import jax.numpy as jnp
from jax import lax
from jax.experimental import pallas as pl
from jax.experimental.pallas import tpu as pltpu
from jax.sharding import PartitionSpec as P

Q = 128
EARLY = 3
STRAIGHT = 0
SCALE_AT = 1
HIGH = lax.Precision.HIGHEST
F32 = jnp.float32
BF16 = jnp.bfloat16
MESH = pl.DeviceIdType.MESH


def mm(a, b, ca, cb):
    return lax.dot_general(a, b, (((ca,), (cb,)), ((), ())), preferred_element_type=F32)


def split(v):
    hi = v.astype(BF16)
    return hi, (v - hi.astype(F32)).astype(BF16)


def lanes(*parts):
    return jnp.concatenate(parts, axis=1)


def rows(*parts):
    return jnp.concatenate(parts, axis=0)


def kernel(cfg, rate_ref, skip_ref, len_in, x_in, dt_in, b_in, c_in, g_in, *refs):
    n_ctx, n_head, hops, fused, ndoc, hopping, early = cfg
    mixed_ref, gx_ref, gdt_ref, gb_ref, gc_ref = refs[:5]
    len_ref, x_ref, dt_ref, b_ref, c_ref, g_ref, load_sem = refs[5:12]
    (s_ref, gz_ref, ddt_ref, out_s, out_g, in_s, in_g, ctx_send, ctx_recv) = refs[12:21]
    if fused:
        part, pair_in, near, hop1_out, hop1_in, hop2_out, hop2_in, chip_in = refs[21:29]
        far, far_in, turn_out, turn_in, scaled, other_scaled, halves = refs[29:36]
        pair_send, pair_recv, hop_send, hop_recv, chip_send, chip_recv, far_send, far_recv, scaled_sem, cross_send, cross_recv = refs[36:]
    width_p = x_ref.shape[1]
    local = x_ref.shape[2]
    width_n = b_ref.shape[0]
    blocks = local // Q
    chunks = blocks // 2
    each = width_n // n_head
    me = lax.axis_index("ctx")
    head = lax.axis_index("head")
    chips = n_head // 2
    core = lax.rem(head, 2)
    chip = head // 2
    mate = {"head": chip * 2 + 1 - core}

    barrier = pltpu.get_barrier_semaphore()

    def beside(step, cross):
        to = {"ctx": me + step}
        if cross:
            to.update(mate)
        return to

    for cross in range(2 if fused else 1):

        @pl.when(me > 0)
        def _():
            pl.semaphore_signal(barrier, inc=1, device_id=beside(-1, cross), device_id_type=MESH)

        @pl.when(me < n_ctx - 1)
        def _():
            pl.semaphore_signal(barrier, inc=1, device_id=beside(1, cross), device_id_type=MESH)

    if fused:
        pl.semaphore_signal(barrier, inc=1, device_id=mate, device_id_type=MESH)
        for d in range(1, chips):
            to = lax.rem(chip + d, chips) * 2 + core
            pl.semaphore_signal(barrier, inc=1, device_id={"head": to}, device_id_type=MESH)

    pairs = (
        (dt_in, dt_ref),
        (len_in, len_ref),
        (x_in, x_ref),
        (b_in, b_ref),
        (g_in, g_ref),
        (c_in, c_ref),
    )
    loads = [
        pltpu.make_async_copy(src, dst, load_sem.at[i]) for i, (src, dst) in enumerate(pairs)
    ]
    for load in loads:
        load.start()

    rate = rate_ref[0]
    skip = skip_ref[0]
    offset = me * local

    row_i = lax.broadcasted_iota(jnp.int32, (Q, Q), 0)
    col_j = lax.broadcasted_iota(jnp.int32, (Q, Q), 1)
    lower = row_i >= col_j
    lower_ones = lower.astype(F32)
    loads[0].wait()
    dt8 = rows(*[dt_ref[0:1, k * Q : (k + 1) * Q] for k in range(blocks)])
    log8 = -rate * dt8
    log_hi, log_rest = log8.astype(BF16), log8 - log8.astype(BF16).astype(F32)
    log_parts = lanes(log_hi, *split(log_rest))
    ones3 = lanes(*[lower.astype(BF16)] * 3)
    cum8 = mm(log_parts, ones3, 1, 1)
    cum_t = mm(ones3, log_parts, 1, 1)
    end8 = cum8[:, Q - 1 : Q]

    loads[1].wait()
    ends = []
    total = len_ref[0]
    for j in range(ndoc - 1):
        ends.append(total)
        total = total + len_ref[j + 1]

    def segment_of(pos):
        seg = jnp.zeros(pos.shape, jnp.int32)
        for end in ends:
            seg = seg + (pos >= end).astype(jnp.int32)
        return seg

    pos8 = (
        offset
        + lax.broadcasted_iota(jnp.int32, (blocks, Q), 0) * Q
        + lax.broadcasted_iota(jnp.int32, (blocks, Q), 1)
    )
    pos_t = (
        offset
        + lax.broadcasted_iota(jnp.int32, (Q, blocks), 1) * Q
        + lax.broadcasted_iota(jnp.int32, (Q, blocks), 0)
    )
    seg8 = segment_of(pos8)
    seg_t = segment_of(pos_t)
    before8 = jnp.where(pos8 == 0, -1, segment_of(pos8 - 1))
    prev8 = before8[:, 0:1]
    last8 = seg8[:, Q - 1 : Q]
    first8 = seg8 == before8[0:1, 0:1]

    din8 = jnp.where(seg8 == prev8, jnp.exp(cum8), 0.0)
    wdt8 = jnp.where(seg8 == last8, jnp.exp(end8 - cum8), 0.0) * dt8
    dall8 = jnp.where(last8 == prev8, jnp.exp(end8), 0.0)

    def cut(ref, k):
        return ref[0, :, k * Q : (k + 1) * Q]

    def cut2(ref, k):
        return ref[:, k * Q : (k + 1) * Q]

    ahead = [None] * blocks
    prod = jnp.ones((1, 1), F32)
    for k in range(blocks):
        ahead[k] = prod
        prod = prod * dall8[k : k + 1]
    decay_dev = prod
    behind = [None] * blocks
    prod = jnp.ones((1, 1), F32)
    for k in reversed(range(blocks)):
        behind[k] = prod
        prod = prod * dall8[k : k + 1]

    @pl.when(me == 0)
    def _():
        in_s[...] = jnp.zeros_like(in_s)

    @pl.when(me == n_ctx - 1)
    def _():
        in_g[...] = jnp.zeros_like(in_g)

    at_end = (me == 0) | (me == n_ctx - 1)
    peers = chips if fused else 0
    beside_count = 2 if fused else 1

    def meet():
        @pl.when(at_end)
        def _():
            pl.semaphore_wait(barrier, peers + beside_count)

        @pl.when(jnp.logical_not(at_end))
        def _():
            pl.semaphore_wait(barrier, peers + 2 * beside_count)

    def mate_copy(src, dst, send, recv):
        return pltpu.make_async_remote_copy(
            src_ref=src,
            dst_ref=dst,
            send_sem=send,
            recv_sem=recv,
            device_id=mate,
            device_id_type=MESH,
        )

    def ctx_copy(r, way):
        src, dst = (out_s, in_s) if way == 0 else (out_g, in_g)
        return pltpu.make_async_remote_copy(
            src_ref=src.at[r],
            dst_ref=dst.at[r],
            send_sem=ctx_send.at[r, way],
            recv_sem=ctx_recv.at[r, way],
            device_id=beside((1, -1)[way], 0),
            device_id_type=MESH,
        )

    def cross_copy(way):
        src, dst = (out_s, in_s) if way == 0 else (out_g, in_g)
        return pltpu.make_async_remote_copy(
            src_ref=src.at[0],
            dst_ref=dst.at[1],
            send_sem=cross_send.at[way],
            recv_sem=cross_recv.at[way],
            device_id=beside((1, -1)[way], 1),
            device_id_type=MESH,
        )

    def hand_copy(way):
        ref = (in_s, in_g)[way]
        return mate_copy(ref.at[0], ref.at[1], cross_send.at[way], cross_recv.at[way])

    def each_way(leaving, act):
        here = (me < n_ctx - 1, me > 0) if leaving else (me > 0, me < n_ctx - 1)
        for way in range(2):

            @pl.when(here[way])
            def _():
                act(way)

    def ctx_start(r):
        each_way(True, lambda way: ctx_copy(r, way).start())

    def ctx_wait(r):
        each_way(False, lambda way: ctx_copy(r, way).wait_recv())

    def ctx_done(r):
        each_way(True, lambda way: ctx_copy(r, way).wait_send())

    def cross_start():
        @pl.when(core == 0)
        def _():
            each_way(True, lambda way: cross_copy(way).start())

    def hand_over():
        ctx_wait(0)

        @pl.when(core == 1)
        def _():
            each_way(False, lambda way: hand_copy(way).start())

    def cross_wait():
        each_way(False, lambda way: cross_copy(way).wait_recv())

    def cross_done():
        @pl.when(core == 0)
        def _():
            each_way(True, lambda way: cross_copy(way).wait_send())

        @pl.when(core == 1)
        def _():
            each_way(False, lambda way: hand_copy(way).wait_send())

    def scaled_copy():
        return mate_copy(scaled, other_scaled, scaled_sem.at[0], scaled_sem.at[1])

    def pair_copy(chunk):
        return mate_copy(
            part.at[chunk, 1 - core], pair_in.at[chunk], pair_send.at[0], pair_recv.at[chunk]
        )

    first_off = jnp.where(chip == 0, 1, chip)
    offs = (first_off, jnp.where(first_off == 1, 2, 1), jnp.where(first_off == 3, 2, 3))

    def chip_copy(chunk, i):
        to = chip ^ offs[i]
        return pltpu.make_async_remote_copy(
            src_ref=near.at[chunk, to],
            dst_ref=chip_in.at[0, offs[i] - 1],
            send_sem=chip_send.at[0],
            recv_sem=chip_recv.at[0],
            device_id={"head": to * 2 + core},
            device_id_type=MESH,
        )

    def far_copy(chunk, i):
        to = chip ^ offs[i]
        return pltpu.make_async_remote_copy(
            src_ref=far.at[to, chunk],
            dst_ref=far_in.at[chunk, offs[i] - 1],
            send_sem=far_send.at[0],
            recv_sem=far_recv.at[chunk],
            device_id={"head": to * 2 + core},
            device_id_type=MESH,
        )

    def turn_copy(chunk, way):
        return pltpu.make_async_remote_copy(
            src_ref=turn_out.at[chunk, way],
            dst_ref=turn_in.at[chunk, way],
            send_sem=far_send.at[0],
            recv_sem=far_recv.at[chunk],
            device_id={"head": (chip ^ (1 + way)) * 2 + core},
            device_id_type=MESH,
        )

    def far_all(ref, chunk):
        return mate_copy(ref.at[chunk], ref.at[chunk], far_send.at[0], far_recv.at[chunk])

    def hop_copy(chunk, hop, way):
        src, dst = (hop1_out, hop1_in) if hop == 0 else (hop2_out, hop2_in)
        to = chip ^ (1 + (way + hop) % 2)
        return pltpu.make_async_remote_copy(
            src_ref=src.at[chunk, way],
            dst_ref=dst.at[chunk, way],
            send_sem=hop_send.at[hop],
            recv_sem=hop_recv.at[chunk, hop],
            device_id={"head": to * 2 + core},
            device_id_type=MESH,
        )

    def hop_both(chunk, hop):
        dst = hop1_in if hop == 0 else hop2_in
        return mate_copy(dst.at[chunk], dst.at[chunk], hop_send.at[hop], hop_recv.at[chunk, hop])

    loads[2].wait()
    loads[3].wait()
    loads[4].wait()
    loads[5].wait()
    state = jnp.zeros((width_p, width_n), F32)
    carry = jnp.zeros((width_p, width_n), F32)
    for k in range(blocks):
        s_ref[k] = state
        b_k = cut2(b_ref, k)
        hi, lo = split(cut(x_ref, k).astype(F32) * wdt8[k : k + 1])
        both = mm(rows(hi, lo), b_k, 1, 1)
        state = dall8[k : k + 1] * state + (both[:width_p] + both[width_p:])
        j = blocks - 1 - k
        gz_ref[j] = carry
        c_j = cut2(c_ref, j)
        hi, lo = split(cut(g_ref, j).astype(F32) * din8[j : j + 1])
        both = mm(rows(hi, lo), c_j, 1, 1)
        carry = dall8[j : j + 1] * carry + (both[:width_p] + both[width_p:])
    out_s[0] = state
    out_g[0] = carry
    meet()
    ctx_start(0)
    if fused:
        cross_start()

    def put(k, way, value):
        if fused:
            chunk, lo = k // 2, (k % 2) * Q
            for h in range(n_head):
                for half in range(2):
                    row = half * each + way * (each // 2)
                    at = (slice(row, row + each // 2), slice(lo, lo + Q))
                    row = h * each + half * (each // 2)
                    part[(chunk, h % 2, h // 2) + at] = value[row : row + each // 2]
        else:
            ref = (gb_ref, gc_ref)[way]
            ref[:, k * Q : (k + 1) * Q] = value

    def scale(k):
        to_start = cut(g_ref, k).astype(F32) * (din8[k : k + 1] * ahead[k])
        to_end = cut(x_ref, k).astype(F32) * (wdt8[k : k + 1] * behind[k])
        scaled[:, k * Q : (k + 1) * Q] = jnp.where(first8[k : k + 1], to_start, to_end)

    def local_w(k):
        x_k, g_k, b_k, c_k = cut(x_ref, k), cut(g_ref, k), cut2(b_ref, k), cut2(c_ref, k)
        mask = lower & (seg_t[:, k : k + 1] == seg8[k : k + 1])
        gap = jnp.where(mask, cum_t[:, k : k + 1] - cum8[k : k + 1], 0.0)
        ddt = jnp.where(mask, jnp.exp(gap), 0.0) * dt8[k : k + 1]
        ddt_ref[k] = ddt
        w_hi, w_lo = split(mm(g_k, x_k, 0, 0) * ddt)
        grad_b = mm(lanes(c_k, c_k), rows(w_hi, w_lo), 1, 0)
        grad_c = mm(lanes(b_k, b_k), lanes(w_hi, w_lo), 1, 1)
        if k < blocks - 1:
            z_hi, z_lo = split(gz_ref[k])
            grad_b += mm(rows(z_hi, z_lo), rows(x_k, x_k), 0, 0) * wdt8[k : k + 1]
        if k > 0:
            s_hi, s_lo = split(s_ref[k])
            grad_c += mm(rows(s_hi, s_lo), rows(g_k, g_k), 0, 0) * din8[k : k + 1]
        put(k, 0, grad_b)
        put(k, 1, grad_c)

    def far_w(k, state_in, grad_in):
        x_k, g_k = cut(x_ref, k), cut(g_ref, k)
        at = slice(k * Q, (k + 1) * Q)
        z_hi, z_lo = split(grad_in)
        s_hi, s_lo = split(state_in)
        wdt, din = wdt8[k : k + 1] * behind[k], din8[k : k + 1] * ahead[k]
        gb_ref[:, at] += mm(rows(z_hi, z_lo), rows(x_k, x_k), 0, 0) * wdt
        gc_ref[:, at] += mm(rows(s_hi, s_lo), rows(g_k, g_k), 0, 0) * din

    diffs, qs, tails = [None] * blocks, [None] * blocks, [None] * blocks

    def halve():
        hi, lo = split(rows(scaled[...], other_scaled[...]))
        halves[0] = hi
        halves[1] = lo

    def turned(ref):
        both = rows(ref[0], ref[1]).T
        low = [both[2 * h * each : (2 * h + 1) * each] for h in range(chips)]
        high = [both[(2 * h + 1) * each : (2 * h + 2) * each] for h in range(chips)]
        return jnp.where(core == 0, rows(*low), rows(*high))

    def chunk_first(chunk):
        return lanes(*[first8[k : k + 1].astype(F32) for k in (2 * chunk, 2 * chunk + 1)]) > 0

    def reach(chunk, states):
        at = slice(chunk * 2 * Q, (chunk + 1) * 2 * Q)
        hi, lo = halves[0, :, at], halves[1, :, at]
        both = mm(states, rows(hi, lo, hi), 1, 0)
        half = width_n // 2
        first = chunk_first(chunk)
        if chunk < early:
            value = jnp.where(first, both[half:], both[:half])
            for h in range(chips):
                far[h, chunk] = value[h * each : (h + 1) * each]

            @pl.when(core == 1)
            def _():
                for way in range(2):
                    turn_out[chunk, way, 0] = far[chip ^ (1 + way), chunk, half_of(way)]
                    turn_out[chunk, way, 1] = far[chip ^ 3, chunk, half_of(way)]
                    turn_copy(chunk, way).start()

            return
        pair_copy(chunk).wait_recv()
        sums = jnp.where(first, 0.0, both[:half]), jnp.where(first, both[half:], 0.0)
        for h in range(chips):
            for way in range(2):
                row = h * each + way * (each // 2)
                more = rows(*[value[row : row + each // 2] for value in sums])
                at = (h, of(way))
                near[(chunk,) + at] = part[(chunk, core) + at] + pair_in[(chunk,) + at] + more

    def outer(k, state_in, grad_in):
        x_k, g_k, b_k, c_k = cut(x_ref, k), cut(g_ref, k), cut2(b_ref, k), cut2(c_ref, k)
        s_k = s_ref[k] + ahead[k] * state_in
        gz = gz_ref[k] + behind[k] * grad_in
        if k + 1 < blocks:
            s_end = s_ref[k + 1] + ahead[k + 1] * state_in
        else:
            s_end = out_s[0] + decay_dev * state_in
        tails[k] = jnp.sum(jnp.sum(gz * s_end, axis=0, keepdims=True), axis=1, keepdims=True)
        a_hi, a_lo = split(mm(c_k, b_k, 0, 0) * ddt_ref[k])
        s_hi, s_lo = split(s_k)
        z_hi, z_lo = split(gz)
        din, wdt = din8[k : k + 1], wdt8[k : k + 1]
        y = mm(lanes(x_k, x_k), lanes(a_hi, a_lo), 1, 1)
        y = y + mm(lanes(s_hi, s_lo), rows(c_k, c_k), 1, 0) * din
        v = mm(lanes(g_k, g_k), rows(a_hi, a_lo), 1, 0)
        v = v + mm(lanes(z_hi, z_lo), rows(b_k, b_k), 1, 0) * wdt
        x_f, g_f = x_k.astype(F32), g_k.astype(F32)
        mixed_ref[0, :, k * Q : (k + 1) * Q] = (y + skip * x_f).astype(BF16)
        gx_ref[0, :, k * Q : (k + 1) * Q] = (v + skip * g_f).astype(BF16)
        q_k = jnp.sum(x_f * v, axis=0, keepdims=True)
        qs[k] = q_k
        diffs[k] = jnp.sum(g_f * y, axis=0, keepdims=True) - q_k

    def of(way):
        return slice(way * each, (way + 1) * each)

    def half_of(way):
        return slice(way * (each // 2), (way + 1) * (each // 2))

    def second(chunk):
        pair_copy(chunk).wait_recv()
        near[chunk] = part[chunk, core] + pair_in[chunk]
        leave(chunk)

    def leave(chunk):
        for way in range(2):
            hop1_out[chunk, way, 0] = near[chunk, chip ^ (1 + way), of(way)]
            hop1_out[chunk, way, 1] = near[chunk, chip ^ 3, of(way)]
            hop_copy(chunk, 0, way).start()

    def third(chunk):
        hop_both(chunk, 0).wait_recv()
        if chunk < early:

            @pl.when(core == 1)
            def _():
                far_all(turn_in, chunk).wait_recv()

        for way in range(2):
            to = chip ^ (2 - way)
            value = near[chunk, to, of(way)] + hop1_in[chunk, way, 1]
            hop2_out[chunk, way] = value
            if chunk < early:

                @pl.when(core == 1)
                def _():
                    more = far[to, chunk, half_of(way)] + turn_in[chunk, way, 1]
                    first = chunk_first(chunk)
                    both = rows(jnp.where(first, 0.0, more), jnp.where(first, more, 0.0))
                    hop2_out[chunk, way] = value + both

            hop_copy(chunk, 1, way).start()

    def last(chunk):
        if chunk < early:
            last_of(chunk, False)
            return

        @pl.when(core == 0)
        def _():
            last_of(chunk, True)

        @pl.when(core == 1)
        def _():
            last_of(chunk, False)

    def last_of(chunk, straight):
        if straight:
            whole = chip_in.at[0]
            mate_copy(whole, whole, chip_send.at[0], chip_recv.at[0]).wait_recv()
            total = near[chunk, chip]
            for d in range(1, chips):
                total = total + chip_in[0, d - 1]
            sums = [total[of(way)] for way in range(2)]
        else:
            hop_both(chunk, 1).wait_recv()
            sums = [
                near[chunk, chip, of(way)] + hop1_in[chunk, way, 0] + hop2_in[chunk, way]
                for way in range(2)
            ]

        def finish(more):
            at = slice(chunk * 2 * Q, (chunk + 1) * 2 * Q)
            first = chunk_first(chunk)
            for way, value in enumerate(sums):
                to_b, to_c = value[: each // 2], value[each // 2 :]
                if more is not None:
                    to_b = to_b + jnp.where(first, 0.0, more[half_of(way)])
                    to_c = to_c + jnp.where(first, more[half_of(way)], 0.0)
                gb_ref[half_of(way), at] = to_b
                gc_ref[half_of(way), at] = to_c

        if chunk >= early:
            finish(None)
            return

        @pl.when(core == 0)
        def _():
            far_all(far_in, chunk).wait_recv()
            more = far[chip, chunk]
            for d in range(1, chips):
                more = more + far_in[chunk, d - 1]
            finish(more)

        @pl.when(core == 1)
        def _():
            finish(far[chip, chunk] + rows(turn_in[chunk, 0, 0], turn_in[chunk, 1, 0]))

    def all_sent():
        mate_copy(pair_in, pair_in, pair_send.at[0], pair_recv.at[0]).wait_send()
        scaled_copy().wait_send()
        if early:
            for which, ref in enumerate((far_in, turn_in)):

                @pl.when(core == which)
                def _():
                    mate_copy(ref, ref, far_send.at[0], far_recv.at[0]).wait_send()

        for which, count in enumerate((early, chunks)):

            @pl.when(core == which)
            def _():
                for hop, ref in enumerate((hop1_out, hop2_out)):
                    sent = ref.at[0:count]
                    mate_copy(sent, sent, hop_send.at[hop], hop_recv.at[0, 0]).wait_send()

        @pl.when(core == 0)
        def _():
            mate_copy(chip_in, chip_in, chip_send.at[0], chip_recv.at[0]).wait_send()

    if fused:
        for k in range(blocks):
            local_w(k)
            if k % 2 == 1:
                pair_copy(k // 2).start()
            if k == SCALE_AT:
                for j in range(blocks):
                    scale(j)
                scaled_copy().start()
        for chunk in range(early):
            second(chunk)
        scaled_copy().wait_recv()
        halve()
        hand_over()
        cross_wait()
        state_in = in_s[0]
        grad_in = in_g[0]
        hi, lo = split(rows(turned(in_g), turned(in_s)))
        states = lanes(hi, hi, lo)
        def send_late(i):
            @pl.when(core == 0)
            def _():
                chip_copy(chunks - 1, i).start()

            if i == 0:

                @pl.when(core == 1)
                def _():
                    leave(chunks - 1)

        def send_far(chunk, i):
            @pl.when(core == 0)
            def _():
                far_copy(chunk, i).start()

        reach(3, states)
        send_late(0)
        reach(0, states)
        send_far(0, 0)
        reach(1, states)
        send_far(1, 0)
        reach(2, states)
        send_far(2, 0)
        send_late(1)
        send_late(2)
        send_far(0, 1)
        send_far(0, 2)
        send_far(1, 1)
        send_far(1, 2)
        send_far(2, 1)
        send_far(2, 2)
        outer(0, state_in, grad_in)
        outer(1, state_in, grad_in)
        third(0)
        outer(2, state_in, grad_in)
        outer(3, state_in, grad_in)

        @pl.when(core == 1)
        def _():
            third(chunks - 1)

        third(1)
        outer(4, state_in, grad_in)
        outer(5, state_in, grad_in)
        third(2)
        outer(6, state_in, grad_in)
        outer(7, state_in, grad_in)
    else:
        for k in range(blocks):
            local_w(k)
        ctx_wait(0)
        for r in range(1, hops):
            out_s[r] = out_s[0] + decay_dev * in_s[r - 1]
            out_g[r] = out_g[0] + decay_dev * in_g[r - 1]
            ctx_start(r)
            ctx_wait(r)
        state_in = in_s[hops - 1]
        grad_in = in_g[hops - 1]
        for k in range(blocks):
            far_w(k, state_in, grad_in)
            outer(k, state_in, grad_in)

    q8 = rows(*qs)
    r8 = rows(*diffs)
    tail8 = rows(*tails)
    back8 = lax.dot_general(
        r8, lower_ones, (((1,), (0,)), ((), ())), precision=HIGH, preferred_element_type=F32
    )
    gdt8 = q8 / dt8 - rate * (back8 + tail8)
    for k in range(blocks):
        gdt_ref[0:1, k * Q : (k + 1) * Q] = gdt8[k : k + 1]

    for r in range(hops):
        ctx_done(r)
    if fused:
        cross_done()
        for chunk in range(chunks):
            last(chunk)
        all_sent()


def move(*refs):
    count = (len(refs) - 1) // 2
    sem = refs[-1]
    copies = [pltpu.make_async_copy(refs[i], refs[count + i], sem.at[i]) for i in range(count)]
    for copy in copies:
        copy.start()
    for copy in copies:
        copy.wait()


def per_device(n_ctx, n_head, inputs, dt, decay_rate, skip, b_proj, c_proj, lengths, grad_out):
    _, width_p, local = inputs.shape
    width_n = b_proj.shape[0]
    longest = n_ctx * local // 4
    hops = max(1, min(n_ctx - 1, (longest - 2) // local + 1))
    each = width_n // n_head
    blocks = local // Q
    chips = n_head // 2
    chunks = blocks // 2
    fused = each % 16 == 0 and EARLY == 3 and longest <= local and chunks == 4 and chips == 4
    hopping = chunks - STRAIGHT
    early = min(EARLY, hopping)
    vmem = pl.BlockSpec(memory_space=pltpu.VMEM)
    smem = pl.BlockSpec(memory_space=pltpu.SMEM)
    anywhere = pl.BlockSpec(memory_space=pl.ANY)
    result = pltpu.VMEM if fused else jax.ShapeDtypeStruct
    grad_rows = each if fused else width_n
    inward = hops + 1 if fused else hops
    scratch = [
        pltpu.SMEM(lengths.shape, lengths.dtype),
        pltpu.VMEM(inputs.shape, BF16),
        pltpu.VMEM(dt.shape, F32),
        pltpu.VMEM(b_proj.shape, BF16),
        pltpu.VMEM(c_proj.shape, BF16),
        pltpu.VMEM(grad_out.shape, BF16),
        pltpu.SemaphoreType.DMA((6,)),
        pltpu.VMEM((blocks, width_p, width_n), F32),
        pltpu.VMEM((blocks, width_p, width_n), F32),
        pltpu.VMEM((blocks, Q, Q), F32),
        pltpu.VMEM((hops, width_p, width_n), F32),
        pltpu.VMEM((hops, width_p, width_n), F32),
        pltpu.VMEM((inward, width_p, width_n), F32),
        pltpu.VMEM((inward, width_p, width_n), F32),
        pltpu.SemaphoreType.DMA((hops, 2)),
        pltpu.SemaphoreType.DMA((hops, 2)),
    ]
    if fused:
        straight = max(1, chunks - hopping)
        held = max(1, hopping)
        scratch += [
            pltpu.VMEM((chunks, 2, chips, 2 * each, 2 * Q), F32),
            pltpu.VMEM((chunks, chips, 2 * each, 2 * Q), F32),
            pltpu.VMEM((chunks, chips, 2 * each, 2 * Q), F32),
            pltpu.VMEM((held, 2, 2, each, 2 * Q), F32),
            pltpu.VMEM((held, 2, 2, each, 2 * Q), F32),
            pltpu.VMEM((held, 2, each, 2 * Q), F32),
            pltpu.VMEM((held, 2, each, 2 * Q), F32),
            pltpu.VMEM((straight, chips - 1, 2 * each, 2 * Q), F32),
            pltpu.VMEM((chips, max(1, early), each, 2 * Q), F32),
            pltpu.VMEM((max(1, early), chips - 1, each, 2 * Q), F32),
            pltpu.VMEM((max(1, early), 2, 2, each // 2, 2 * Q), F32),
            pltpu.VMEM((max(1, early), 2, 2, each // 2, 2 * Q), F32),
            pltpu.VMEM((width_p, local), F32),
            pltpu.VMEM((width_p, local), F32),
            pltpu.VMEM((2, 2 * width_p, local), BF16),
            pltpu.SemaphoreType.DMA((1,)),
            pltpu.SemaphoreType.DMA((chunks,)),
            pltpu.SemaphoreType.DMA((2,)),
            pltpu.SemaphoreType.DMA((held, 2)),
            pltpu.SemaphoreType.DMA((1,)),
            pltpu.SemaphoreType.DMA((straight,)),
            pltpu.SemaphoreType.DMA((1,)),
            pltpu.SemaphoreType.DMA((max(1, early),)),
            pltpu.SemaphoreType.DMA((2,)),
            pltpu.SemaphoreType.DMA((2,)),
            pltpu.SemaphoreType.DMA((2,)),
        ]
    mixed, gx, gdt, gb, gc = pl.pallas_call(
        functools.partial(kernel, (n_ctx, n_head, hops, fused, lengths.shape[0], hopping, early)),
        out_shape=(
            result(inputs.shape, BF16),
            result(inputs.shape, BF16),
            result(dt.shape, F32),
            result((grad_rows, local), F32),
            result((grad_rows, local), F32),
        ),
        in_specs=[smem, smem] + [anywhere] * 6,
        out_specs=(vmem,) * 5,
        scratch_shapes=scratch,
        compiler_params=pltpu.CompilerParams(collective_id=0, has_side_effects=True),
    )(decay_rate, skip, lengths, inputs, dt, b_proj, c_proj, grad_out)
    if not fused:
        gb = lax.psum_scatter(gb, "head", scatter_dimension=0, tiled=True)
        gc = lax.psum_scatter(gc, "head", scatter_dimension=0, tiled=True)
    results = (mixed, gx, gdt, gb, gc)
    if fused:
        results = tuple(pltpu.with_memory_space_constraint(r, pltpu.VMEM) for r in results)
    return pl.pallas_call(
        move,
        out_shape=tuple(jax.ShapeDtypeStruct(r.shape, r.dtype) for r in results),
        in_specs=[vmem if fused else anywhere] * 5,
        out_specs=(anywhere,) * 5,
        scratch_shapes=[pltpu.SemaphoreType.DMA((5,))],
    )(*results)


def solution(mesh):
    return jax.shard_map(
        functools.partial(per_device, mesh.shape["ctx"], mesh.shape["head"]),
        mesh=mesh,
        in_specs=(
            P("head", None, "ctx"),
            P("head", "ctx"),
            P("head"),
            P("head"),
            P(None, "ctx"),
            P(None, "ctx"),
            P(),
            P("head", None, "ctx"),
        ),
        out_specs=(
            P("head", None, "ctx"),
            P("head", None, "ctx"),
            P("head", "ctx"),
            P("head", "ctx"),
            P("head", "ctx"),
        ),
        check_vma=False,
    )
```
